128 devices in a mesh: seg: 4 (over z_lo, core), batch: 32 (over z_hi, y, x).
Axes of the slice: x: 4, y: 4, z: 4 (z_hi: 2, z_lo: 2; z = z_hi * 2 + z_lo), core: 2. Of those that a mesh axis runs over, the one named last changes fastest.
Arguments:
- starts: float32 [4, 4096, 1024], P('seg', 'batch'), may hold values from -6 to 6
- targets: float32 [4, 4096, 1024], P('seg', 'batch'), may hold values from -6 to 6
- counts: int32 [4], P('seg'), may hold values from 1 to 3, as said below
- w_in: bfloat16 [1024, 1024], P('batch'), may hold values from -0.1875 to 0.1875
- b_in: float32 [1024], replicated, may hold values from -3 to 3
- w_out: bfloat16 [1024, 1024], P('batch'), may hold values from -0.1875 to 0.1875
Outputs:
- grad_starts: float32 [4, 4096, 1024], P('seg', 'batch')
- grad_w_in: float32 [1024, 1024], P('batch')
- grad_w_out: float32 [1024, 1024], P('batch')
- grad_b_in: float32 [1024], P('batch')
The draws below stay inside these ranges and needn't reach their ends.
Inputs may be any that keep to these rules, and one draw needn't show every extreme that they name: `counts`: some segment takes 3 steps and some takes 1.
All inputs are finite; a program needn't handle non-finite values.
Results may differ from the reference program's by a relative error of at most 0.00125.
Values may be sent and summed in bfloat16 or wider, within the bound.
No kernel may reach another device: no remote copies, remote signals or barrier semaphores. Data moves between devices by JAX's collectives and lax.ppermute only.
A program may use at most 64 MiB of HBM per device.

```python
import math
import jax
import jax.numpy as jnp
from jax import lax

D = 1024
H = 1024
MAXSTEP = 3
SEGS = 4
TRAJ = 4096


def draw_counts(key, part):
    picked = jax.random.randint(jax.random.fold_in(key, 11), (SEGS,), 1, MAXSTEP + 1)
    shuffled = jax.random.permutation(jax.random.fold_in(key, 12), SEGS)
    picked = picked.at[shuffled[0]].set(MAXSTEP)
    picked = picked.at[shuffled[1]].set(1)
    return picked.astype(jnp.int32)


def steps_of(own_key, dims, pieces, smallest, high):
    def one(axis_at, parts):
        steps = jax.random.uniform(jax.random.fold_in(jax.random.fold_in(own_key, 6), axis_at), (parts,), jnp.float32, smallest / len(pieces), high / len(pieces))
        return jnp.repeat(jnp.exp(steps), dims[axis_at] // parts).reshape((-1,) + (1,) * (len(dims) - axis_at - 1))

    factor_of = one(*pieces[0])
    for cut in pieces[1:]:
        factor_of = factor_of * one(*cut)
    return factor_of


def normal_values(key, shape, scale, reach, pieces=(), held_as=jnp.bfloat16):
    level = steps_of(key, shape, pieces, -0.22, 0.18) if pieces else 1.0
    drawn = jax.random.normal(key, shape, jnp.float32) * scale * level
    return jnp.minimum(jnp.maximum(drawn, -reach), reach).astype(held_as)


def setup_inputs(seed: int = 0) -> dict:
    arg_keys = jax.random.split(jax.random.key(seed), 7)
    starts = normal_values(arg_keys[0], (SEGS, TRAJ, D), 1.0, 6.0, ((0, 4), (1, 32)), jnp.float32)
    targets = normal_values(arg_keys[1], (SEGS, TRAJ, D), 1.0, 6.0, ((0, 4), (1, 32)), jnp.float32)
    counts = draw_counts(jax.random.fold_in(arg_keys[6], 71), 0)
    w_in = normal_values(arg_keys[3], (D, H), D ** -0.5, 0.1875, ((0, 32),))
    b_in = normal_values(arg_keys[4], (H,), 0.5, 3.0, (), jnp.float32)
    w_out = normal_values(arg_keys[5], (H, D), H ** -0.5, 0.1875, ((0, 32),))
    return {"starts": starts, "targets": targets, "counts": counts, "w_in": w_in, "b_in": b_in, "w_out": w_out}


time_step = 0.25
penalty = 1.0

def contract_rows(left, right):
    return lax.dot_general(left, right, (((0,), (0,)), ((), ())), preferred_element_type=jnp.float32)

def contract_cols(left, right):
    return lax.dot_general(left, right, (((1,), (1,)), ((), ())), preferred_element_type=jnp.float32)

def vector_field(current, w_in, b_in, w_out):
    inputs = current.astype(jnp.bfloat16)
    hidden = jnp.tanh(jnp.dot(inputs, w_in, preferred_element_type=jnp.float32) + b_in)
    slope = jnp.dot(hidden.astype(jnp.bfloat16), w_out, preferred_element_type=jnp.float32)
    return (slope, inputs, hidden)

def runge_kutta(current, w_in, b_in, w_out):
    slope_one, in_one, hid_one = vector_field(current, w_in, b_in, w_out)
    slope_two, in_two, hid_two = vector_field(current + 0.5 * time_step * slope_one, w_in, b_in, w_out)
    slope_three, in_three, hid_three = vector_field(current + 0.5 * time_step * slope_two, w_in, b_in, w_out)
    slope_four, in_four, hid_four = vector_field(current + time_step * slope_three, w_in, b_in, w_out)
    updated = current + time_step / 6.0 * (slope_one + 2.0 * slope_two + 2.0 * slope_three + slope_four)
    inputs = jnp.stack([in_one, in_two, in_three, in_four])
    hiddens = jnp.stack([hid_one, hid_two, hid_three, hid_four])
    return (updated, inputs, hiddens)

def field_back(hidden, outer, w_in, w_out):
    outer_low = outer.astype(jnp.bfloat16)
    inner = contract_cols(outer_low, w_out) * (1.0 - hidden * hidden)
    inner_low = inner.astype(jnp.bfloat16)
    return (contract_cols(inner_low, w_in), outer_low, inner_low, lax.optimization_barrier(jnp.sum(inner, axis=0)))

def runge_kutta_back(state_bar, inputs, hiddens, w_in, w_out):
    back_four, outer_four, inner_four, bias_four = field_back(hiddens[3], time_step / 6.0 * state_bar, w_in, w_out)
    back_three, outer_three, inner_three, bias_three = field_back(hiddens[2], time_step / 3.0 * state_bar + time_step * back_four, w_in, w_out)
    back_two, outer_two, inner_two, bias_two = field_back(hiddens[1], time_step / 3.0 * state_bar + 0.5 * time_step * back_three, w_in, w_out)
    back_one, outer_one, inner_one, bias_one = field_back(hiddens[0], time_step / 6.0 * state_bar + 0.5 * time_step * back_two, w_in, w_out)
    new_bar = state_bar + back_one + back_two + back_three + back_four
    outers = jnp.concatenate([outer_one, outer_two, outer_three, outer_four], axis=0)
    inners = jnp.concatenate([inner_one, inner_two, inner_three, inner_four], axis=0)
    flat_inputs = inputs.reshape(-1, inputs.shape[-1])
    flat_hidden = hiddens.astype(jnp.bfloat16).reshape(-1, hiddens.shape[-1])
    grad_in_step = contract_rows(flat_inputs, inners)
    grad_out_step = contract_rows(flat_hidden, outers)
    grad_bias_step = bias_one + bias_two + bias_three + bias_four
    return (new_bar, grad_in_step, grad_out_step, grad_bias_step)

def integrate_segment(start, step_total, w_in, b_in, w_out):
    saved_empty = jnp.zeros((MAXSTEP,) + start.shape, jnp.float32)

    def advance(step_index, carry):
        current, saved = carry
        saved = lax.dynamic_update_index_in_dim(saved, current, step_index, 0)
        updated, inputs, hiddens = runge_kutta(current, w_in, b_in, w_out)
        return (updated, saved)
    return lax.fori_loop(0, step_total, advance, (start, saved_empty))

def back_segment(end_bar, saved, step_total, w_in, b_in, w_out):
    initial = (end_bar, jnp.zeros(w_in.shape, jnp.float32), jnp.zeros(w_out.shape, jnp.float32), jnp.zeros(b_in.shape, jnp.float32))

    def retreat(turn, carry):
        state_bar, acc_in, acc_out, acc_bias = carry
        step_index = step_total - 1 - turn
        current = lax.dynamic_index_in_dim(saved, step_index, 0, keepdims=False)
        updated, inputs, hiddens = runge_kutta(current, w_in, b_in, w_out)
        new_bar, grad_in_step, grad_out_step, grad_bias_step = runge_kutta_back(state_bar, inputs, hiddens, w_in, w_out)
        return (new_bar, acc_in + grad_in_step, acc_out + grad_out_step, acc_bias + grad_bias_step)
    return lax.fori_loop(0, step_total, retreat, initial)

def reference(starts, targets, counts, w_in, b_in, w_out):
    ends = []
    saves = []
    for segment in range(SEGS):
        end_state, saved = integrate_segment(starts[segment], counts[segment], w_in, b_in, w_out)
        ends.append(end_state)
        saves.append(saved)
    gaps = []
    for segment in range(SEGS):
        if segment < SEGS - 1:
            gaps.append(ends[segment] - starts[segment + 1])
        else:
            gaps.append(jnp.zeros_like(ends[segment]))
    total_in = jnp.zeros(w_in.shape, jnp.float32)
    total_out = jnp.zeros(w_out.shape, jnp.float32)
    total_bias = jnp.zeros(b_in.shape, jnp.float32)
    start_grads = []
    for segment in range(SEGS):
        end_bar = ends[segment] - targets[segment] + penalty * gaps[segment]
        start_bar, grad_in_seg, grad_out_seg, grad_bias_seg = back_segment(end_bar, saves[segment], counts[segment], w_in, b_in, w_out)
        total_in = total_in + grad_in_seg
        total_out = total_out + grad_out_seg
        total_bias = total_bias + grad_bias_seg
        if segment > 0:
            start_grads.append(start_bar + -(penalty * gaps[segment - 1]))
        else:
            start_grads.append(start_bar)
    scale = 1.0 / math.sqrt(TRAJ)
    return (jnp.stack(start_grads), total_in * scale, total_out * scale, total_bias * scale)
```

```python
import math

import jax
import jax.numpy as jnp
from jax import lax
from jax.sharding import Mesh, PartitionSpec as P

D = 1024
MAXSTEP = 3
time_step = 0.25
penalty = 1.0
SEG = ("zlo", "core")
GROUP = ("zlo", "batch")


def contract_rows(left, right):
    return lax.dot_general(
        left, right, (((0,), (0,)), ((), ())), preferred_element_type=jnp.float32
    )


def contract_cols(left, right):
    return lax.dot_general(
        left, right, (((1,), (1,)), ((), ())), preferred_element_type=jnp.float32
    )


def vector_field(current, w_in, b_in, w_out):
    inputs = current.astype(jnp.bfloat16)
    hidden = jnp.tanh(jnp.dot(inputs, w_in, preferred_element_type=jnp.float32) + b_in)
    slope = jnp.dot(hidden.astype(jnp.bfloat16), w_out, preferred_element_type=jnp.float32)
    return (slope, inputs, hidden)


def runge_kutta(current, w_in, b_in, w_out):
    slope_one, in_one, hid_one = vector_field(current, w_in, b_in, w_out)
    slope_two, in_two, hid_two = vector_field(
        current + 0.5 * time_step * slope_one, w_in, b_in, w_out
    )
    slope_three, in_three, hid_three = vector_field(
        current + 0.5 * time_step * slope_two, w_in, b_in, w_out
    )
    slope_four, in_four, hid_four = vector_field(
        current + time_step * slope_three, w_in, b_in, w_out
    )
    updated = current + time_step / 6.0 * (
        slope_one + 2.0 * slope_two + 2.0 * slope_three + slope_four
    )
    inputs = jnp.stack([in_one, in_two, in_three, in_four])
    hiddens = jnp.stack([hid_one, hid_two, hid_three, hid_four])
    return (updated, inputs, hiddens)


def field_back(hidden, outer, w_in, w_out):
    outer_low = outer.astype(jnp.bfloat16)
    inner = contract_cols(outer_low, w_out) * (1.0 - hidden * hidden)
    inner_low = inner.astype(jnp.bfloat16)
    return (contract_cols(inner_low, w_in), outer_low, inner_low, jnp.sum(inner, axis=0))


def runge_kutta_back(state_bar, inputs, hiddens, w_in, w_out):
    back_four, outer_four, inner_four, bias_four = field_back(
        hiddens[3], time_step / 6.0 * state_bar, w_in, w_out
    )
    back_three, outer_three, inner_three, bias_three = field_back(
        hiddens[2], time_step / 3.0 * state_bar + time_step * back_four, w_in, w_out
    )
    back_two, outer_two, inner_two, bias_two = field_back(
        hiddens[1], time_step / 3.0 * state_bar + 0.5 * time_step * back_three, w_in, w_out
    )
    back_one, outer_one, inner_one, bias_one = field_back(
        hiddens[0], time_step / 6.0 * state_bar + 0.5 * time_step * back_two, w_in, w_out
    )
    new_bar = state_bar + back_one + back_two + back_three + back_four
    outers = jnp.concatenate([outer_one, outer_two, outer_three, outer_four], axis=0)
    inners = jnp.concatenate([inner_one, inner_two, inner_three, inner_four], axis=0)
    flat_inputs = inputs.reshape(-1, inputs.shape[-1])
    flat_hidden = hiddens.astype(jnp.bfloat16).reshape(-1, hiddens.shape[-1])
    grad_in_step = contract_rows(flat_inputs, inners)
    grad_out_step = contract_rows(flat_hidden, outers)
    grad_bias_step = bias_one + bias_two + bias_three + bias_four
    return (new_bar, grad_in_step, grad_out_step, grad_bias_step)


def level_of(peak):
    return jnp.ceil(256.0 * jnp.log2(jnp.maximum(peak, 1e-36))) + 2.0


def coded(values, level):
    scaled = values * (32767.0 * jnp.exp2(level * (-1.0 / 256.0)))
    return scaled


def low(values):
    return jnp.round(values).astype(jnp.int32).astype(jnp.int16)


def shift_seg(block, distance):
    route = [(i - distance, i) for i in range(4) if 0 <= i - distance < 4]
    return lax.ppermute(block, SEG, route)


def body(starts, targets, counts, w_in, b_in, w_out):
    start_now = starts[0]
    target_now = targets[0]
    step_total = counts[0]
    core = lax.axis_index("core")
    seg_place = lax.axis_index(SEG)
    batch_count = lax.axis_size("batch")
    row_count = start_now.shape[0]
    own = w_in.shape[0]

    next_start = shift_seg(start_now, -1)
    shard = jnp.where(core == 0, w_in, w_out)
    gathered = lax.all_to_all(
        jnp.broadcast_to(shard[None], (batch_count, own, D)), "batch", 0, 0
    ).reshape(D, D)
    both = lax.all_to_all(jnp.broadcast_to(gathered[None], (2, D, D)), "core", 0, 0)
    full_in, full_out = both[0], both[1]

    def advance_plain(step_index, carry):
        current, saved = carry
        saved = lax.dynamic_update_index_in_dim(saved, current, step_index, 0)
        updated, inputs, hiddens = runge_kutta(current, full_in, b_in, full_out)
        return (updated, saved)

    saved_empty = jnp.zeros((MAXSTEP, row_count, D), jnp.float32)
    end_state, saved = lax.fori_loop(0, step_total, advance_plain, (start_now, saved_empty))

    def recall(step_index):
        current = lax.dynamic_index_in_dim(saved, step_index, 0, keepdims=False)
        updated, inputs, hiddens = runge_kutta(current, full_in, b_in, full_out)
        return (inputs, hiddens)

    previous = shift_seg(end_state, 1)
    has_next = (seg_place < 3).astype(jnp.float32)
    has_prev = (seg_place > 0).astype(jnp.float32)
    end_bar = (end_state - target_now) + penalty * ((end_state - next_start) * has_next)

    def retreat(turn, carry):
        state_bar, acc_in, acc_out, acc_bias = carry
        step_index = step_total - 1 - turn
        inputs, hiddens = recall(step_index)
        new_bar, grad_in_step, grad_out_step, grad_bias_step = runge_kutta_back(
            state_bar, inputs, hiddens, full_in, full_out
        )
        return (new_bar, acc_in + grad_in_step, acc_out + grad_out_step, acc_bias + grad_bias_step)

    initial = (
        end_bar,
        jnp.zeros(full_in.shape, jnp.float32),
        jnp.zeros(full_out.shape, jnp.float32),
        jnp.zeros(b_in.shape, jnp.float32),
    )
    start_bar, total_in, total_out, total_bias = lax.fori_loop(0, step_total, retreat, initial)
    gap_before = (previous - start_now) * has_prev
    grad_starts = (start_bar - penalty * gap_before)[None]

    keep = jnp.where(core == 0, total_in, total_out)
    send = jnp.where(core == 0, total_out, total_in)
    total = keep + lax.ppermute(send, "core", [(0, 1), (1, 0)])
    group = lax.axis_size(GROUP)
    piece = D // group
    level = level_of(jnp.max(jnp.abs(total), axis=0, keepdims=True))
    data = low(coded(total, level)).reshape(group, piece, D)
    bias_level = level_of(jnp.max(jnp.abs(total_bias)))
    bias_scaled = coded(total_bias, bias_level)
    bias_high = jnp.round(bias_scaled)
    bias_rows = jnp.stack([bias_high, (bias_scaled - bias_high) * 32767.0]).reshape(2, batch_count, own)
    bias_rows = jnp.pad(jnp.swapaxes(bias_rows, 0, 1), ((0, 0), (0, 0), (0, D - own)))
    head = jnp.concatenate(
        [
            jnp.broadcast_to(level[None], (batch_count, 1, D)),
            jnp.broadcast_to(bias_level, (batch_count, 1, D)),
            bias_rows,
            jnp.zeros((batch_count, 4, D), jnp.float32),
        ],
        axis=1,
    )
    head = jnp.repeat(low(head), group // batch_count, axis=0)
    data = jnp.swapaxes(data.reshape(batch_count, 2, piece, D), 0, 1).reshape(group, piece, D)
    head = jnp.swapaxes(head.reshape(batch_count, 2, 8, D), 0, 1).reshape(group, 8, D)
    got = lax.all_to_all(jnp.concatenate([data, head], axis=1), GROUP, 0, 0)
    got = got.astype(jnp.float32)
    back = jnp.exp2(got[:, piece : piece + 1] * (1.0 / 256.0)) * (1.0 / 32767.0)
    part = jnp.sum(got[:, :piece] * back, axis=0)
    bias_back = jnp.exp2(got[:, piece + 1] * (1.0 / 256.0)) * (1.0 / 32767.0)
    bias_part = jnp.sum(
        (got[:, piece + 2] + got[:, piece + 3] * (1.0 / 32767.0)) * bias_back, axis=0
    )
    mine = jnp.concatenate([part, jnp.broadcast_to(bias_part[None], (8, D))], axis=0)
    four = lax.all_to_all(jnp.broadcast_to(mine[None], (4, piece + 8, D)), SEG, 0, 0)
    scale = 1.0 / math.sqrt(row_count * batch_count)
    four = four * scale
    grad_in = jnp.concatenate([four[0, :piece], four[2, :piece]], axis=0)
    grad_out = jnp.concatenate([four[1, :piece], four[3, :piece]], axis=0)
    grad_bias = four[0, piece, :own] + four[1, piece, :own]
    return (grad_starts, grad_in, grad_out, grad_bias)


def solution(mesh):
    segs, batches = mesh.devices.shape
    finer = Mesh(mesh.devices.reshape(2, segs // 2, batches), ("zlo", "core", "batch"))
    return jax.shard_map(
        body,
        mesh=finer,
        in_specs=(
            P(SEG, "batch", None),
            P(SEG, "batch", None),
            P(SEG),
            P("batch", None),
            P(),
            P("batch", None),
        ),
        out_specs=(P(SEG, "batch", None), P("batch", None), P("batch", None), P("batch")),
        check_vma=False,
    )
```

```python
import math

import jax
import jax.numpy as jnp
from jax import lax
from jax.experimental import pallas as pl
from jax.experimental.pallas import tpu as pltpu
from jax.sharding import Mesh, PartitionSpec as P

MAXSTEP = 3
STAGES = 4
step_size = 0.25
penalty = 1.0
SEG = ("zlo", "core")
GROUP = ("zlo", "batch")
f32 = jnp.float32
bf16 = jnp.bfloat16
LANES = 128
HEAD = 16
TOP = 32767.0
VMEM = pl.BlockSpec(memory_space=pltpu.VMEM)
ANY = pl.BlockSpec(memory_space=pl.ANY)
SMEM = pl.BlockSpec(memory_space=pltpu.SMEM)


def product(left, right):
    return jnp.dot(left, right, preferred_element_type=f32)


def integrate_kernel(
    info, start, target, following, bias_in, own_w, other_w,
    ends, bar, bias, left, right,
    w, w_turned, state, tanhs, total, sems,
):
    count, core, has_next = info[0], info[1], info[2].astype(f32)
    slot_in = 1 - core
    slot_out = core
    rows = start.shape[0]
    first = pltpu.make_async_copy(own_w, w.at[core], sems.at[0])
    second = pltpu.make_async_copy(other_w, w.at[1 - core], sems.at[1])
    first.start()
    second.start()
    state[...] = start[...]
    bias[...] = jnp.zeros_like(bias)
    offset = bias_in[...]
    first.wait()
    second.wait()
    w_turned[0] = w[0].T
    w_turned[1] = w[1].T

    def place(at):
        return pl.ds(pl.multiple_of(at * rows, rows), rows)

    def field(u, at):
        inputs = u.astype(bf16)
        left[slot_in, place(at), :] = inputs
        hidden = jnp.tanh(product(inputs, w[0]) + offset)
        tanhs[at] = hidden
        low = hidden.astype(bf16)
        left[slot_out, place(at), :] = low
        return product(low, w[1])

    def field_back(q, at):
        outer = q.astype(bf16)
        right[slot_out, place(at), :] = outer
        hidden = tanhs[at]
        inner = product(outer, w_turned[1]) * (1.0 - hidden * hidden)
        bias[...] += jnp.sum(inner, axis=0, keepdims=True)
        low = inner.astype(bf16)
        right[slot_in, place(at), :] = low
        return product(low, w_turned[0])

    def forward(s, carry):
        at = STAGES * s
        k = field(state[...], at)
        total[...] = k
        k = field(state[...] + 0.5 * step_size * k, at + 1)
        total[...] += 2.0 * k
        k = field(state[...] + 0.5 * step_size * k, at + 2)
        total[...] += 2.0 * k
        k = field(state[...] + step_size * k, at + 3)
        state[...] = state[...] + step_size / 6.0 * (total[...] + k)
        return carry

    lax.fori_loop(0, count, forward, 0)
    end = state[...]
    ends[...] = end
    state[...] = (end - target[...]) + penalty * ((end - following[...]) * has_next)

    def backward(turn, carry):
        at = STAGES * (count - 1 - turn)
        g = field_back(step_size / 6.0 * state[...], at + 3)
        total[...] = state[...] + g
        g = field_back(step_size / 3.0 * state[...] + step_size * g, at + 2)
        total[...] += g
        g = field_back(step_size / 3.0 * state[...] + 0.5 * step_size * g, at + 1)
        total[...] += g
        g = field_back(step_size / 6.0 * state[...] + 0.5 * step_size * g, at)
        state[...] = total[...] + g
        return carry

    lax.fori_loop(0, count, backward, 0)
    bar[...] = state[...]

    def clear(s, carry):
        block = pl.ds(pl.multiple_of(s * STAGES * rows, STAGES * rows), STAGES * rows)
        for slot in range(2):
            left[slot, block, :] = jnp.zeros((STAGES * rows, left.shape[2]), bf16)
            right[slot, block, :] = jnp.zeros((STAGES * rows, right.shape[2]), bf16)
        return carry

    lax.fori_loop(count, MAXSTEP, clear, 0)


def integrate(info, start, target, following, bias_in, own_w, other_w):
    rows, width = start.shape
    depth = own_w.shape[1]
    factors = jax.ShapeDtypeStruct((2, MAXSTEP * STAGES * rows, width), bf16)
    states = jax.ShapeDtypeStruct((rows, width), f32)
    return pl.pallas_call(
        integrate_kernel,
        out_shape=(states, states, jax.ShapeDtypeStruct((1, depth), f32), factors, factors),
        in_specs=[SMEM] + [VMEM] * 4 + [ANY] * 2,
        out_specs=(VMEM,) * 5,
        scratch_shapes=[
            pltpu.VMEM((2, width, depth), bf16),
            pltpu.VMEM((2, depth, width), bf16),
            pltpu.VMEM((rows, width), f32),
            pltpu.VMEM((MAXSTEP * STAGES, rows, depth), f32),
            pltpu.VMEM((rows, width), f32),
            pltpu.SemaphoreType.DMA((2,)),
        ],
        compiler_params=pltpu.CompilerParams(vmem_limit_bytes=40 * 1024 * 1024),
        name="integrate",
    )(info, start, target, following, bias_in, own_w, other_w)


def level_of(peak):
    return jnp.ceil(256.0 * jnp.log2(jnp.maximum(peak, 1e-30))) + 1.0


def scale_of(level):
    return jnp.exp2(level * (1.0 / 256.0) - 15.0)


def steps_of(level):
    return jnp.exp2(15.0 - level * (1.0 / 256.0))


def whole(values):
    return jnp.round(values).astype(jnp.int32).astype(jnp.int16)


def code_kernel(keep, received, bias, message):
    halves, owners, height, _ = message.shape
    piece = keep.shape[0] // (halves * owners)
    blocks = keep.shape[1] // LANES
    row = lax.broadcasted_iota(jnp.int32, (HEAD, LANES), 0)
    bias_now = bias[...]
    bias_level = level_of(jnp.abs(bias_now))
    bias_steps = bias_now * steps_of(bias_level)
    bias_high = jnp.round(bias_steps)
    bias_low = (bias_steps - bias_high) * TOP
    base = jnp.where(row == 8, bias_level, 0.0)
    base = jnp.where(row == 9, bias_high, base)
    base = jnp.where(row == 10, bias_low, base)
    for owner in range(owners):
        for half in range(halves):
            at = (owner * halves + half) * piece
            head = base
            for block in range(blocks):
                columns = pl.ds(block * LANES, LANES)
                values = keep[pl.ds(at, piece), columns] + received[pl.ds(at, piece), columns]
                level = level_of(jnp.max(jnp.abs(values), axis=0, keepdims=True))
                head = jnp.where(row == block, level, head)
                message[half, owner, pl.ds(block * piece, piece), :] = whole(
                    values * steps_of(level)
                )
            message[half, owner, pl.ds(blocks * piece, HEAD), :] = whole(head)


def code(keep, received, bias, halves, batches):
    depth, width = keep.shape
    steps = width // LANES
    owners = batches // steps
    piece = depth // (halves * batches)
    height = piece * steps + HEAD
    block = pl.BlockSpec((depth // steps, width), lambda i: (i, 0))
    return pl.pallas_call(
        code_kernel,
        grid=(steps,),
        out_shape=jax.ShapeDtypeStruct((halves, batches, height, LANES), jnp.int16),
        in_specs=[block, block, pl.BlockSpec((1, LANES), lambda i: (0, i))],
        out_specs=pl.BlockSpec((halves, owners, height, LANES), lambda i: (0, i, 0, 0)),
        compiler_params=pltpu.CompilerParams(vmem_limit_bytes=16 * 1024 * 1024),
        name="code",
    )(keep, received, bias)


def decode_kernel(message, out):
    senders, height, _ = message.shape
    blocks = out.shape[1] // LANES
    piece = (height - HEAD) // blocks

    @pl.when(pl.program_id(0) == 0)
    def _():
        out[...] = jnp.zeros_like(out)

    sums = [jnp.zeros((piece, LANES), f32) for _ in range(blocks)]
    bias = jnp.zeros((1, LANES), f32)
    for sender in range(senders):
        head = message[sender, pl.ds(blocks * piece, HEAD), :].astype(jnp.int32).astype(f32)
        scale = scale_of(head)
        bias += (head[9:10] + head[10:11] * (1.0 / TOP)) * scale[8:9]
        for block in range(blocks):
            data = message[sender, pl.ds(block * piece, piece), :].astype(jnp.int32).astype(f32)
            sums[block] += data * scale[block : block + 1]
    for block in range(blocks):
        out[pl.ds(0, piece), pl.ds(block * LANES, LANES)] += sums[block]
    out[pl.ds(piece, 8), pl.ds(0, LANES)] += jnp.broadcast_to(bias, (8, LANES))


def decode(message, width):
    senders, height, _ = message.shape
    steps = 8
    piece = (height - HEAD) * LANES // width
    return pl.pallas_call(
        decode_kernel,
        grid=(steps,),
        out_shape=jax.ShapeDtypeStruct((piece + 8, width), f32),
        in_specs=[pl.BlockSpec((senders // steps, height, LANES), lambda i: (i, 0, 0))],
        out_specs=pl.BlockSpec((piece + 8, width), lambda i: (0, 0)),
        compiler_params=pltpu.CompilerParams(vmem_limit_bytes=16 * 1024 * 1024),
        name="decode",
    )(message)


def contract_rows(left, right):
    return lax.dot_general(left, right, (((0,), (0,)), ((), ())), preferred_element_type=f32)


def shift_seg(block, distance):
    count = lax.axis_size(SEG)
    route = [(i - distance, i) for i in range(count) if 0 <= i - distance < count]
    return lax.ppermute(block, SEG, route)


def swap(block):
    return lax.ppermute(block, "core", [(0, 1), (1, 0)])


def body(starts, targets, counts, w_in, b_in, w_out):
    start = starts[0]
    core = lax.axis_index("core")
    place = lax.axis_index(SEG)
    batches = lax.axis_size("batch")
    halves = lax.axis_size("zlo")
    rows, width = start.shape
    own = w_in.shape[0]

    following = shift_seg(start, -1)
    shard = jnp.where(core == 0, w_in, w_out)
    own_w = lax.all_to_all(jnp.broadcast_to(shard[None], (batches, own, width)), "batch", 0, 0)
    own_w = own_w.reshape(batches * own, width)
    other_w = swap(own_w)

    has_next = (place < lax.axis_size(SEG) - 1).astype(jnp.int32)
    info = jnp.stack([counts[0], core, has_next])
    ends, bar, bias, left, right = integrate(
        info, start, targets[0], following, b_in[None], own_w, other_w
    )
    previous = shift_seg(ends, 1)
    has_prev = (place > 0).astype(f32)
    grad_starts = (bar - penalty * ((previous - start) * has_prev))[None]

    received = swap(contract_rows(left[0], right[0]))
    keep = contract_rows(left[1], right[1])
    message = code(keep, received, bias, halves, batches)
    message = lax.all_to_all(message.reshape((halves * batches,) + message.shape[2:]), GROUP, 0, 0)
    mine = decode(message, width)
    four = lax.all_to_all(jnp.broadcast_to(mine[None], (4,) + mine.shape), SEG, 0, 0)
    piece = mine.shape[0] - 8
    four = four * (1.0 / math.sqrt(rows * batches))
    grad_in = jnp.concatenate([four[0, :piece], four[2, :piece]], axis=0)
    grad_out = jnp.concatenate([four[1, :piece], four[3, :piece]], axis=0)
    bias_rows = four[0, piece, :LANES] + four[1, piece, :LANES]
    offset = lax.axis_index("batch") % (LANES // own) * own
    grad_bias = lax.dynamic_slice(bias_rows, (offset,), (own,))
    return (grad_starts, grad_in, grad_out, grad_bias)


def solution(mesh):
    segs, batches = mesh.devices.shape
    finer = Mesh(mesh.devices.reshape(2, segs // 2, batches), ("zlo", "core", "batch"))
    return jax.shard_map(
        body,
        mesh=finer,
        in_specs=(
            P(SEG, "batch", None),
            P(SEG, "batch", None),
            P(SEG),
            P("batch", None),
            P(),
            P("batch", None),
        ),
        out_specs=(P(SEG, "batch", None), P("batch", None), P("batch", None), P("batch")),
        check_vma=False,
    )
```

```python
import functools
import math

import jax
import jax.numpy as jnp
from jax import lax
from jax.experimental import pallas as pl
from jax.experimental.pallas import tpu as pltpu
from jax.sharding import Mesh, PartitionSpec as P


MAXSTEP = 3
STAGES = 4
step_size = 0.25
penalty = 1.0
SEG = ("zlo", "core")
GROUP = ("zlo", "batch")
f32 = jnp.float32
bf16 = jnp.bfloat16
LANES = 128
HEAD = 8
TOP = 32767.0
VMEM = pl.BlockSpec(memory_space=pltpu.VMEM)
ANY = pl.BlockSpec(memory_space=pl.ANY)
SMEM = pl.BlockSpec(memory_space=pltpu.SMEM)


def product(left, right):
    return jnp.dot(left, right, preferred_element_type=f32)


def integrate_kernel(
    info, given, bias_in, own_w, other_w,
    ends, bar, bias, left, right,
    w, w_turned, state, tanhs, total, sems,
):
    count, core, has_next = info[0], info[1], info[2].astype(f32)
    slot_in = 1 - core
    slot_out = core
    rows = state.shape[0]
    middle = right.shape[3]
    first = pltpu.make_async_copy(own_w, w.at[core], sems.at[0])
    second = pltpu.make_async_copy(other_w, w.at[1 - core], sems.at[1])
    first.start()
    second.start()
    state[...] = given[0]
    bias[...] = jnp.zeros_like(bias)
    offset = bias_in[...]
    first.wait()
    second.wait()
    w_turned[0] = w[0].T
    w_turned[1] = w[1].T

    def place(at):
        return pl.ds(pl.multiple_of(at * rows, rows), rows)

    def field(u, at):
        inputs = u.astype(bf16)
        left[slot_in, place(at), :] = inputs
        hidden = jnp.tanh(product(inputs, w[0]) + offset)
        tanhs[at] = hidden
        low = hidden.astype(bf16)
        left[slot_out, place(at), :] = low
        return product(low, w[1])

    def field_back(q, at):
        outer = q.astype(bf16)
        right[slot_out, 0, place(at), :] = outer[:, :middle]
        right[slot_out, 1, place(at), :] = outer[:, middle:]
        hidden = tanhs[at]
        inner = product(outer, w_turned[1]) * (1.0 - hidden * hidden)
        bias[...] += jnp.sum(inner, axis=0, keepdims=True)
        low = inner.astype(bf16)
        right[slot_in, 0, place(at), :] = low[:, :middle]
        right[slot_in, 1, place(at), :] = low[:, middle:]
        return product(low, w_turned[0])

    def forward(s, carry):
        at = STAGES * s
        k = field(state[...], at)
        total[...] = k
        k = field(state[...] + 0.5 * step_size * k, at + 1)
        total[...] += 2.0 * k
        k = field(state[...] + 0.5 * step_size * k, at + 2)
        total[...] += 2.0 * k
        k = field(state[...] + step_size * k, at + 3)
        state[...] = state[...] + step_size / 6.0 * (total[...] + k)
        return carry

    lax.fori_loop(0, count, forward, 0)
    end = state[...]
    ends[...] = end
    state[...] = (end - given[1]) + penalty * ((end - given[2]) * has_next)

    def backward(turn, carry):
        at = STAGES * (count - 1 - turn)
        g = field_back(step_size / 6.0 * state[...], at + 3)
        total[...] = state[...] + g
        g = field_back(step_size / 3.0 * state[...] + step_size * g, at + 2)
        total[...] += g
        g = field_back(step_size / 3.0 * state[...] + 0.5 * step_size * g, at + 1)
        total[...] += g
        g = field_back(step_size / 6.0 * state[...] + 0.5 * step_size * g, at)
        state[...] = total[...] + g
        return carry

    lax.fori_loop(0, count, backward, 0)
    bar[...] = state[...]

    def clear(s, carry):
        block = pl.ds(pl.multiple_of(s * STAGES * rows, STAGES * rows), STAGES * rows)
        for slot in range(2):
            left[slot, block, :] = jnp.zeros((STAGES * rows, left.shape[2]), bf16)
            for half in range(2):
                right[slot, half, block, :] = jnp.zeros((STAGES * rows, middle), bf16)
        return carry

    lax.fori_loop(count, MAXSTEP, clear, 0)


def integrate(info, given, bias_in, own_w, other_w):
    _, rows, width = given.shape
    depth = own_w.shape[1]
    terms = MAXSTEP * STAGES * rows
    lefts = jax.ShapeDtypeStruct((2, terms, width), bf16)
    rights = jax.ShapeDtypeStruct((2, 2, terms, width // 2), bf16)
    states = jax.ShapeDtypeStruct((rows, width), f32)
    return pl.pallas_call(
        integrate_kernel,
        out_shape=(states, states, jax.ShapeDtypeStruct((1, depth), f32), lefts, rights),
        in_specs=[SMEM] + [VMEM] * 2 + [ANY] * 2,
        out_specs=(VMEM,) * 5,
        scratch_shapes=[
            pltpu.VMEM((2, width, depth), bf16),
            pltpu.VMEM((2, depth, width), bf16),
            pltpu.VMEM((rows, width), f32),
            pltpu.VMEM((MAXSTEP * STAGES, rows, depth), f32),
            pltpu.VMEM((rows, width), f32),
            pltpu.SemaphoreType.DMA((2,)),
        ],
        compiler_params=pltpu.CompilerParams(vmem_limit_bytes=32 * 1024 * 1024),
        name="integrate",
    )(info, given, bias_in, own_w, other_w)


def level_of(peak):
    return jnp.ceil(256.0 * jnp.log2(jnp.maximum(peak, 1e-30))) + 1.0


def scale_of(level):
    return jnp.exp2(level * (1.0 / 256.0) - 15.0)


def steps_of(level):
    return jnp.exp2(15.0 - level * (1.0 / 256.0))


def whole(values):
    return jnp.round(values).astype(jnp.int32).astype(jnp.int16)


def code_kernel(keep_low, keep_high, received_low, received_high, bias, message):
    halves, owners, _, _ = message.shape
    piece = keep_low.shape[0] // (halves * owners)
    shared = keep_low.shape[1] // LANES
    blocks = 2 * shared
    row = lax.broadcasted_iota(jnp.int32, (HEAD, LANES), 0)
    bias_now = bias[...]
    bias_level = level_of(jnp.abs(bias_now))
    bias_steps = bias_now * steps_of(bias_level)
    bias_high = jnp.round(bias_steps)
    bias_low = (bias_steps - bias_high) * TOP
    head = jnp.where(row == shared, bias_level, 0.0)
    head = jnp.where(row == shared + 1, bias_high, head)
    head = jnp.where(row == shared + 2, bias_low, head)
    for block in range(shared):
        columns = pl.ds(block * LANES, LANES)
        pair = (
            keep_low[:, columns] + received_low[:, columns],
            keep_high[:, columns] + received_high[:, columns],
        )
        peak = jnp.maximum(jnp.abs(pair[0]), jnp.abs(pair[1]))
        level = level_of(jnp.max(peak, axis=0, keepdims=True))
        steps = steps_of(level)
        head = jnp.where(row == block, level, head)
        for part, values in zip((block, block + shared), pair):
            numbers = whole(values * steps)
            for owner in range(owners):
                for half in range(halves):
                    at = (owner * halves + half) * piece
                    message[half, owner, pl.ds(part * piece, piece), :] = numbers[at : at + piece]
    numbers = whole(head)
    for owner in range(owners):
        for half in range(halves):
            message[half, owner, pl.ds(blocks * piece, HEAD), :] = numbers


def code(keep, received, bias, halves, batches):
    depth, width = keep[0].shape[0], 2 * keep[0].shape[1]
    steps = width // LANES
    owners = batches // steps
    piece = depth // (halves * batches)
    height = piece * steps + HEAD
    return pl.pallas_call(
        code_kernel,
        grid=(steps,),
        out_shape=jax.ShapeDtypeStruct((halves, batches, height, LANES), jnp.int16),
        in_specs=[pl.BlockSpec((depth // steps, width // 2), lambda i: (i, 0))] * 4
        + [pl.BlockSpec((1, LANES), lambda i: (0, i))],
        out_specs=pl.BlockSpec((halves, owners, height, LANES), lambda i: (0, i, 0, 0)),
        compiler_params=pltpu.CompilerParams(vmem_limit_bytes=16 * 1024 * 1024),
        name="code",
    )(*keep, *received, bias)


def decode_kernel(message, out):
    senders, height, _ = message.shape
    blocks = out.shape[1] // LANES
    shared = blocks // 2
    piece = (height - HEAD) // blocks

    @pl.when(pl.program_id(0) == 0)
    def _():
        out[...] = jnp.zeros_like(out)

    sums = [jnp.zeros((piece, LANES), f32) for _ in range(blocks)]
    bias = jnp.zeros((1, LANES), f32)
    for sender in range(senders):
        head = message[sender, pl.ds(blocks * piece, HEAD), :].astype(jnp.int32).astype(f32)
        scale = scale_of(head)
        high, low = head[shared + 1 : shared + 2], head[shared + 2 : shared + 3]
        bias += (high + low * (1.0 / TOP)) * scale[shared : shared + 1]
        for block in range(blocks):
            data = message[sender, pl.ds(block * piece, piece), :].astype(jnp.int32).astype(f32)
            at = block % shared
            sums[block] += data * scale[at : at + 1]
    for block in range(blocks):
        out[pl.ds(0, piece), pl.ds(block * LANES, LANES)] += sums[block]
    out[pl.ds(piece, 8), pl.ds(0, LANES)] += jnp.broadcast_to(bias, (8, LANES))


def decode(message, width):
    senders, height, _ = message.shape
    steps = 8
    piece = (height - HEAD) * LANES // width
    return pl.pallas_call(
        decode_kernel,
        grid=(steps,),
        out_shape=jax.ShapeDtypeStruct((piece + 8, width), f32),
        in_specs=[pl.BlockSpec((senders // steps, height, LANES), lambda i: (i, 0, 0))],
        out_specs=pl.BlockSpec((piece + 8, width), lambda i: (0, 0)),
        compiler_params=pltpu.CompilerParams(vmem_limit_bytes=16 * 1024 * 1024),
        name="decode",
    )(message)


def lay_out_kernel(scale, info, mine, by_core, by_zlo, by_both, grad_in, grad_out, grad_bias):
    core, zlo, offset = info[0], info[1], info[2]
    piece = mine.shape[0] - 8
    here = pl.ds(pl.multiple_of(zlo * piece, piece), piece)
    there = pl.ds(pl.multiple_of((1 - zlo) * piece, piece), piece)
    rows = pl.ds(0, piece)

    def fill(kept, other):
        kept[here, :] = mine[rows, :] * scale
        kept[there, :] = by_zlo[rows, :] * scale
        other[here, :] = by_core[rows, :] * scale
        other[there, :] = by_both[rows, :] * scale

    @pl.when(core == 0)
    def _():
        fill(grad_in, grad_out)

    @pl.when(core == 1)
    def _():
        fill(grad_out, grad_in)

    stretch = (mine[pl.ds(piece, 8), pl.ds(0, LANES)] + by_core[pl.ds(piece, 8), pl.ds(0, LANES)]) * scale
    grad_bias[...] = pltpu.roll(stretch, LANES - offset, 1)


def lay_out(scale, info, *quarters):
    rows, width = quarters[0].shape
    gradient = jax.ShapeDtypeStruct((2 * (rows - 8), width), f32)
    return pl.pallas_call(
        functools.partial(lay_out_kernel, scale),
        out_shape=(gradient, gradient, jax.ShapeDtypeStruct((8, LANES), f32)),
        in_specs=[SMEM] + [VMEM] * 4,
        out_specs=(VMEM,) * 3,
        compiler_params=pltpu.CompilerParams(vmem_limit_bytes=8 * 1024 * 1024),
        name="lay_out",
    )(info, *quarters)


def contract_rows(left, right):
    return lax.dot_general(left, right, (((0,), (0,)), ((), ())), preferred_element_type=f32)


def shift_seg(block, distance):
    count = lax.axis_size(SEG)
    route = [(i - distance, i) for i in range(count) if 0 <= i - distance < count]
    return lax.ppermute(block, SEG, route)


def swap(block):
    return lax.ppermute(block, "core", [(0, 1), (1, 0)])


def body(starts, targets, counts, w_in, b_in, w_out):
    start = starts[0]
    core = lax.axis_index("core")
    place = lax.axis_index(SEG)
    batches = lax.axis_size("batch")
    halves = lax.axis_size("zlo")
    rows, width = start.shape
    own = w_in.shape[0]

    following = shift_seg(start, -1)
    shard = jnp.where(core == 0, w_in, w_out)
    copies = jnp.broadcast_to(shard[None], (batches, own, width))
    own_w = lax.all_to_all(copies, "batch", 0, 0)
    own_w = own_w.reshape(batches * own, width)
    other_w = swap(own_w)
    given = jnp.stack([start, targets[0], following])

    has_next = (place < lax.axis_size(SEG) - 1).astype(jnp.int32)
    info = jnp.stack([counts[0], core, has_next])
    ends, bar, bias, left, right = integrate(info, given, b_in[None], own_w, other_w)
    previous = shift_seg(ends, 1)
    has_prev = (place > 0).astype(f32)
    grad_starts = (bar - penalty * ((previous - start) * has_prev))[None]

    received, keep = [], []
    for half in range(2):
        sent = contract_rows(left[0], right[0, half])
        received.append(swap(sent))
    for half in range(2):
        keep.append(contract_rows(left[1], right[1, half]))
    message = code(keep, received, bias, halves, batches)
    message = lax.all_to_all(message.reshape((halves * batches,) + message.shape[2:]), GROUP, 0, 0)
    mine = decode(message, width)
    quarters = [mine] + [
        lax.ppermute(mine, SEG, [(i, i ^ flip) for i in range(4)]) for flip in (1, 2, 3)
    ]
    offset = lax.axis_index("batch") % (LANES // own) * own
    places = jnp.stack([core, lax.axis_index("zlo"), offset])
    scale = 1.0 / math.sqrt(rows * batches)
    grad_in, grad_out, grad_bias = lay_out(scale, places, *quarters)
    return (grad_starts, grad_in, grad_out, grad_bias[0, :own])


def solution(mesh):
    segs, batches = mesh.devices.shape
    finer = Mesh(mesh.devices.reshape(2, segs // 2, batches), ("zlo", "core", "batch"))
    return jax.shard_map(
        body,
        mesh=finer,
        in_specs=(
            P(SEG, "batch", None),
            P(SEG, "batch", None),
            P(SEG),
            P("batch", None),
            P(),
            P("batch", None),
        ),
        out_specs=(P(SEG, "batch", None), P("batch", None), P("batch", None), P("batch")),
        check_vma=False,
    )
```

```python
import functools
import math

import jax
import jax.numpy as jnp
from jax import lax
from jax.experimental import pallas as pl
from jax.experimental.pallas import tpu as pltpu
from jax.sharding import Mesh, PartitionSpec as P


MAXSTEP = 3
STAGES = 4
step_size = 0.25
penalty = 1.0
SEG = ("zlo", "core")
f32 = jnp.float32
bf16 = jnp.bfloat16
LANES = 128
HEAD = 8
TOP = 32767.0
VMEM = pl.BlockSpec(memory_space=pltpu.VMEM)
ANY = pl.BlockSpec(memory_space=pl.ANY)
SMEM = pl.BlockSpec(memory_space=pltpu.SMEM)


def product(left, right):
    return jnp.dot(left, right, preferred_element_type=f32)


def integrate_kernel(
    info, given, bias_in, own_w, other_w,
    ends, bar, bias, left, right,
    w, w_turned, state, tanhs, total, sems,
):
    count, core, has_next = info[0], info[1], info[2].astype(f32)
    slot_in = 1 - core
    slot_out = core
    rows = state.shape[0]
    middle = right.shape[3]
    first = pltpu.make_async_copy(own_w, w.at[core], sems.at[0])
    second = pltpu.make_async_copy(other_w, w.at[1 - core], sems.at[1])
    first.start()
    second.start()
    state[...] = given[0]
    bias[...] = jnp.zeros_like(bias)
    offset = bias_in[...]
    first.wait()
    second.wait()
    w_turned[0] = w[0].T
    w_turned[1] = w[1].T

    def place(at):
        return pl.ds(pl.multiple_of(at * rows, rows), rows)

    def field(u, at):
        inputs = u.astype(bf16)
        left[slot_in, place(at), :] = inputs
        hidden = jnp.tanh(product(inputs, w[0]) + offset)
        tanhs[at] = hidden
        low = hidden.astype(bf16)
        left[slot_out, place(at), :] = low
        return product(low, w[1])

    def field_back(q, at):
        outer = q.astype(bf16)
        right[slot_out, 0, place(at), :] = outer[:, :middle]
        right[slot_out, 1, place(at), :] = outer[:, middle:]
        hidden = tanhs[at]
        inner = product(outer, w_turned[1]) * (1.0 - hidden * hidden)
        bias[...] += jnp.sum(inner, axis=0, keepdims=True)
        low = inner.astype(bf16)
        right[slot_in, 0, place(at), :] = low[:, :middle]
        right[slot_in, 1, place(at), :] = low[:, middle:]
        return product(low, w_turned[0])

    def forward(s, carry):
        at = STAGES * s
        k = field(state[...], at)
        total[...] = k
        k = field(state[...] + 0.5 * step_size * k, at + 1)
        total[...] += 2.0 * k
        k = field(state[...] + 0.5 * step_size * k, at + 2)
        total[...] += 2.0 * k
        k = field(state[...] + step_size * k, at + 3)
        state[...] = state[...] + step_size / 6.0 * (total[...] + k)
        return carry

    lax.fori_loop(0, count, forward, 0)
    end = state[...]
    ends[...] = end
    state[...] = (end - given[1]) + penalty * ((end - given[2]) * has_next)

    def backward(turn, carry):
        at = STAGES * (count - 1 - turn)
        g = field_back(step_size / 6.0 * state[...], at + 3)
        total[...] = state[...] + g
        g = field_back(step_size / 3.0 * state[...] + step_size * g, at + 2)
        total[...] += g
        g = field_back(step_size / 3.0 * state[...] + 0.5 * step_size * g, at + 1)
        total[...] += g
        g = field_back(step_size / 6.0 * state[...] + 0.5 * step_size * g, at)
        state[...] = total[...] + g
        return carry

    lax.fori_loop(0, count, backward, 0)
    bar[...] = state[...]

    def clear(s, carry):
        block = pl.ds(pl.multiple_of(s * STAGES * rows, STAGES * rows), STAGES * rows)
        for slot in range(2):
            left[slot, block, :] = jnp.zeros((STAGES * rows, left.shape[2]), bf16)
            for half in range(2):
                right[slot, half, block, :] = jnp.zeros((STAGES * rows, middle), bf16)
        return carry

    lax.fori_loop(count, MAXSTEP, clear, 0)


def integrate(info, given, bias_in, own_w, other_w):
    _, rows, width = given.shape
    depth = own_w.shape[1]
    terms = MAXSTEP * STAGES * rows
    lefts = jax.ShapeDtypeStruct((2, terms, width), bf16)
    rights = jax.ShapeDtypeStruct((2, 2, terms, width // 2), bf16)
    states = jax.ShapeDtypeStruct((rows, width), f32)
    return pl.pallas_call(
        integrate_kernel,
        out_shape=(states, states, jax.ShapeDtypeStruct((1, depth), f32), lefts, rights),
        in_specs=[SMEM] + [VMEM] * 2 + [ANY] * 2,
        out_specs=(VMEM,) * 5,
        scratch_shapes=[
            pltpu.VMEM((2, width, depth), bf16),
            pltpu.VMEM((2, depth, width), bf16),
            pltpu.VMEM((rows, width), f32),
            pltpu.VMEM((MAXSTEP * STAGES, rows, depth), f32),
            pltpu.VMEM((rows, width), f32),
            pltpu.SemaphoreType.DMA((2,)),
        ],
        compiler_params=pltpu.CompilerParams(vmem_limit_bytes=32 * 1024 * 1024),
        name="integrate",
    )(info, given, bias_in, own_w, other_w)


def level_of(peak):
    return jnp.ceil(256.0 * jnp.log2(jnp.maximum(peak, 1e-30))) + 1.0


def scale_of(level):
    return jnp.exp2(level * (1.0 / 256.0) - 15.0)


def steps_of(level):
    return jnp.exp2(15.0 - level * (1.0 / 256.0))


def whole(values):
    return jnp.round(values).astype(jnp.int32).astype(jnp.int16)


def head_of(bias):
    level = level_of(jnp.abs(bias))
    steps = bias * steps_of(level)
    high = jnp.round(steps)
    return level, high, (steps - high) * TOP


def code_piece(low, high, head, store, store_head):
    shared = len(low)
    row = lax.broadcasted_iota(jnp.int32, (HEAD, LANES), 0)
    tile = jnp.zeros((HEAD, LANES), f32)
    for at, values in enumerate(head):
        tile = jnp.where(row == shared + at, values, tile)
    for block in range(shared):
        pair = (low[block](), high[block]())
        peak = jnp.maximum(jnp.abs(pair[0]), jnp.abs(pair[1]))
        level = level_of(jnp.max(peak, axis=0, keepdims=True))
        steps = steps_of(level)
        tile = jnp.where(row == block, level, tile)
        store(block, whole(pair[0] * steps))
        store(block + shared, whole(pair[1] * steps))
    store_head(whole(tile))


def code_kernel(batches, keep_low, keep_high, got_low, got_high, bias, message):
    turns = bias.shape[1] // LANES
    owners = batches // turns
    depth = keep_low.shape[0] // turns
    piece = depth // owners
    shared = keep_low.shape[1] // LANES

    def turn(i, carry):
        rows = pl.ds(pl.multiple_of(i * depth, depth), depth)
        stretch = bias[:, pl.ds(pl.multiple_of(i * LANES, LANES), LANES)]

        def sums(kept, got):
            return [
                functools.partial(lambda c: kept[rows, c] + got[rows, c], pl.ds(at * LANES, LANES))
                for at in range(shared)
            ]

        def store(block, numbers):
            for owner in range(owners):
                message[i * owners + owner, pl.ds(block * piece, piece), :] = numbers[
                    owner * piece : (owner + 1) * piece
                ]

        def store_head(numbers):
            for owner in range(owners):
                message[i * owners + owner, pl.ds(2 * shared * piece, HEAD), :] = numbers

        code_piece(
            sums(keep_low, got_low), sums(keep_high, got_high), head_of(stretch), store, store_head
        )
        return carry

    lax.fori_loop(0, turns, turn, 0)


def code(keep, received, bias, batches):
    depth, middle = keep[0].shape
    height = depth // batches * (2 * middle // LANES) + HEAD
    return pl.pallas_call(
        functools.partial(code_kernel, batches),
        out_shape=jax.ShapeDtypeStruct((batches, height, LANES), jnp.int16),
        in_specs=[VMEM] * 5,
        out_specs=VMEM,
        compiler_params=pltpu.CompilerParams(vmem_limit_bytes=16 * 1024 * 1024),
        name="code",
    )(*keep, *received, bias)


def read_piece(blocks, load):
    piece = blocks[0][1]
    shared = len(blocks) // 2
    head = load(len(blocks) * piece, HEAD).astype(jnp.int32).astype(f32)
    scale = scale_of(head)
    high, low = head[shared + 1 : shared + 2], head[shared + 2 : shared + 3]
    bias = (high + low * (1.0 / TOP)) * scale[shared : shared + 1]
    values = []
    for block, (at, rows) in enumerate(blocks):
        share = block % shared
        numbers = load(at, rows).astype(jnp.int32).astype(f32)
        values.append(numbers * scale[share : share + 1])
    return values, bias


def blocks_of(height, count):
    piece = (height - HEAD) // count
    return [(block * piece, piece) for block in range(count)]


def decode_kernel(count, message, out):
    senders, height, _ = message.shape
    blocks = blocks_of(height, count)
    group = 4

    def turn(i, carry):
        bias, *sums = carry
        for j in range(group):
            values, more = read_piece(
                blocks, lambda at, rows: message[i * group + j, pl.ds(at, rows), :]
            )
            bias = bias + more
            sums = [one + other for one, other in zip(sums, values)]
        return (bias, *sums)

    zeros = (jnp.zeros((1, LANES), f32),) + (jnp.zeros((blocks[0][1], LANES), f32),) * count
    bias, *sums = lax.fori_loop(0, senders // group, turn, zeros)
    ready = [functools.partial(lambda v: v, value) for value in sums]

    def store(block, numbers):
        at, rows = blocks[block]
        out[pl.ds(at, rows), :] = numbers

    def store_head(numbers):
        out[pl.ds(height - HEAD, HEAD), :] = numbers

    code_piece(ready[: count // 2], ready[count // 2 :], head_of(bias), store, store_head)


def decode(message, count):
    return pl.pallas_call(
        functools.partial(decode_kernel, count),
        out_shape=jax.ShapeDtypeStruct(message.shape[1:], jnp.int16),
        in_specs=[VMEM],
        out_specs=VMEM,
        compiler_params=pltpu.CompilerParams(vmem_limit_bytes=8 * 1024 * 1024),
        name="decode",
    )(message)


def lay_out_kernel(scale, info, mine, by_core, by_zlo, by_both, grad_in, grad_out, grad_bias):
    core, offset = info[0], info[1]
    count = grad_in.shape[1] // LANES
    blocks = blocks_of(mine.shape[0], count)
    parts = []
    stretches = []
    for ref in (mine, by_core, by_zlo, by_both):
        values, bias = read_piece(
            blocks, functools.partial(lambda r, at, rows: r[pl.ds(at, rows), :], ref)
        )
        parts.append(values)
        stretches.append(bias)

    def fill(kept, other):
        for block in range(count):
            columns = pl.ds(block * LANES, LANES)
            kept[:, columns] = (parts[0][block] + parts[2][block]) * scale
            other[:, columns] = (parts[1][block] + parts[3][block]) * scale

    @pl.when(core == 0)
    def _():
        fill(grad_in, grad_out)

    @pl.when(core == 1)
    def _():
        fill(grad_out, grad_in)

    stretch = ((stretches[0] + stretches[3]) + (stretches[1] + stretches[2])) * scale
    turned = pltpu.roll(jnp.broadcast_to(stretch, (8, LANES)), LANES - offset, 1)
    grad_bias[...] = turned[0:1, : grad_bias.shape[1]]


def lay_out(scale, info, quarters, rows, width):
    gradient = jax.ShapeDtypeStruct((rows, width), f32)
    return pl.pallas_call(
        functools.partial(lay_out_kernel, scale),
        out_shape=(gradient, gradient, jax.ShapeDtypeStruct((1, rows), f32)),
        in_specs=[SMEM] + [VMEM] * 4,
        out_specs=(VMEM,) * 3,
        compiler_params=pltpu.CompilerParams(vmem_limit_bytes=8 * 1024 * 1024),
        name="lay_out",
    )(info, *quarters)


def contract_rows(left, right):
    return lax.dot_general(left, right, (((0,), (0,)), ((), ())), preferred_element_type=f32)


def shift_seg(block, distance):
    count = lax.axis_size(SEG)
    route = [(i - distance, i) for i in range(count) if 0 <= i - distance < count]
    return lax.ppermute(block, SEG, route)


def swap(block):
    return lax.ppermute(block, "core", [(0, 1), (1, 0)])


def body(starts, targets, counts, w_in, b_in, w_out):
    start = starts[0]
    core = lax.axis_index("core")
    place = lax.axis_index(SEG)
    batches = lax.axis_size("batch")
    rows, width = start.shape
    own = w_in.shape[0]

    following = shift_seg(start, -1)
    shard = jnp.where(core == 0, w_in, w_out)
    copies = jnp.broadcast_to(shard[None], (batches, own, width))
    own_w = lax.all_to_all(copies, "batch", 0, 0)
    own_w = own_w.reshape(batches * own, width)
    other_w = swap(own_w)
    given = jnp.stack([start, targets[0], following])

    has_next = (place < lax.axis_size(SEG) - 1).astype(jnp.int32)
    info = jnp.stack([counts[0], core, has_next])
    ends, bar, bias, left, right = integrate(info, given, b_in[None], own_w, other_w)
    previous = shift_seg(ends, 1)
    has_prev = (place > 0).astype(f32)
    grad_starts = (bar - penalty * ((previous - start) * has_prev))[None]

    received, keep = [], []
    for half in range(2):
        sent = contract_rows(left[0], right[0, half])
        received.append(swap(sent))
    for half in range(2):
        keep.append(contract_rows(left[1], right[1, half]))
    message = code(keep, received, bias, batches)
    message = lax.all_to_all(message, "batch", 0, 0)
    mine = decode(message, width // LANES)
    quarters = [mine] + [
        lax.ppermute(mine, SEG, [(i, i ^ flip) for i in range(4)]) for flip in (1, 2, 3)
    ]
    offset = lax.axis_index("batch") % (LANES // own) * own
    scale = 1.0 / math.sqrt(rows * batches)
    grad_in, grad_out, grad_bias = lay_out(scale, jnp.stack([core, offset]), quarters, own, width)
    return (grad_starts, grad_in, grad_out, grad_bias[0])


def solution(mesh):
    segs, batches = mesh.devices.shape
    finer = Mesh(mesh.devices.reshape(2, segs // 2, batches), ("zlo", "core", "batch"))
    return jax.shard_map(
        body,
        mesh=finer,
        in_specs=(
            P(SEG, "batch", None),
            P(SEG, "batch", None),
            P(SEG),
            P("batch", None),
            P(),
            P("batch", None),
        ),
        out_specs=(P(SEG, "batch", None), P("batch", None), P("batch", None), P("batch")),
        check_vma=False,
    )
```

```python
import functools
import math

import jax
import jax.numpy as jnp
from jax import lax
from jax.experimental import pallas as pl
from jax.experimental.pallas import tpu as pltpu
from jax.sharding import Mesh, PartitionSpec as P


MAXSTEP = 3
STAGES = 4
step_size = 0.25
penalty = 1.0
SEG = ("zlo", "core")
f32 = jnp.float32
bf16 = jnp.bfloat16
LANES = 128
HEAD = 8
TOP = 32767.0
VMEM = pl.BlockSpec(memory_space=pltpu.VMEM)
ANY = pl.BlockSpec(memory_space=pl.ANY)
SMEM = pl.BlockSpec(memory_space=pltpu.SMEM)


def product(left, right):
    return jnp.dot(left, right, preferred_element_type=f32)


def integrate_kernel(
    info, given, bias_in, own_w, other_w,
    ends, bar, bias, left, right,
    w, w_turned, state, tanhs, total, sems,
):
    count, core, has_next = info[0], info[1], info[2].astype(f32)
    slot_in = 1 - core
    slot_out = core
    rows = state.shape[0]
    middle = right.shape[3]
    first = pltpu.make_async_copy(own_w, w.at[core], sems.at[0])
    second = pltpu.make_async_copy(other_w, w.at[1 - core], sems.at[1])
    first.start()
    second.start()
    state[...] = given[0]
    bias[...] = jnp.zeros_like(bias)
    offset = bias_in[...]
    first.wait()
    second.wait()

    def place(at):
        return pl.ds(pl.multiple_of(at * rows, rows), rows)

    def field(u, at):
        inputs = u.astype(bf16)
        left[slot_in, place(at), :] = inputs
        hidden = jnp.tanh(product(inputs, w[0]) + offset)
        tanhs[at] = hidden
        low = hidden.astype(bf16)
        left[slot_out, place(at), :] = low
        return product(low, w[1])

    def field_back(q, at):
        outer = q.astype(bf16)
        right[slot_out, 0, place(at), :] = outer[:, :middle]
        right[slot_out, 1, place(at), :] = outer[:, middle:]
        hidden = tanhs[at]
        inner = product(outer, w_turned[1]) * (1.0 - hidden * hidden)
        bias[...] += jnp.sum(inner, axis=0, keepdims=True)
        low = inner.astype(bf16)
        right[slot_in, 0, place(at), :] = low[:, :middle]
        right[slot_in, 1, place(at), :] = low[:, middle:]
        return product(low, w_turned[0])

    def turn(part):
        quarter = w.shape[1] // STAGES
        for which in range(2):
            rows_now = pl.ds(part * quarter, quarter)
            w_turned[which, :, rows_now] = w[which, rows_now, :].T

    def forward(s, carry, beside=lambda part: None):
        at = STAGES * s
        beside(0)
        k = field(state[...], at)
        total[...] = k
        beside(1)
        k = field(state[...] + 0.5 * step_size * k, at + 1)
        total[...] += 2.0 * k
        beside(2)
        k = field(state[...] + 0.5 * step_size * k, at + 2)
        total[...] += 2.0 * k
        beside(3)
        k = field(state[...] + step_size * k, at + 3)
        state[...] = state[...] + step_size / 6.0 * (total[...] + k)
        return carry

    forward(0, 0, turn)
    lax.fori_loop(1, count, forward, 0)
    end = state[...]
    ends[...] = end
    state[...] = (end - given[1]) + penalty * ((end - given[2]) * has_next)

    def backward(turn, carry):
        at = STAGES * (count - 1 - turn)
        g = field_back(step_size / 6.0 * state[...], at + 3)
        total[...] = state[...] + g
        g = field_back(step_size / 3.0 * state[...] + step_size * g, at + 2)
        total[...] += g
        g = field_back(step_size / 3.0 * state[...] + 0.5 * step_size * g, at + 1)
        total[...] += g
        g = field_back(step_size / 6.0 * state[...] + 0.5 * step_size * g, at)
        state[...] = total[...] + g
        return carry

    lax.fori_loop(0, count, backward, 0)
    bar[...] = state[...]

    def clear(s, carry):
        block = pl.ds(pl.multiple_of(s * STAGES * rows, STAGES * rows), STAGES * rows)
        for slot in range(2):
            left[slot, block, :] = jnp.zeros((STAGES * rows, left.shape[2]), bf16)
            for half in range(2):
                right[slot, half, block, :] = jnp.zeros((STAGES * rows, middle), bf16)
        return carry

    lax.fori_loop(count, MAXSTEP, clear, 0)


def integrate(info, given, bias_in, own_w, other_w):
    _, rows, width = given.shape
    depth = own_w.shape[1]
    terms = MAXSTEP * STAGES * rows
    lefts = jax.ShapeDtypeStruct((2, terms, width), bf16)
    rights = jax.ShapeDtypeStruct((2, 2, terms, width // 2), bf16)
    states = jax.ShapeDtypeStruct((rows, width), f32)
    return pl.pallas_call(
        integrate_kernel,
        out_shape=(states, states, jax.ShapeDtypeStruct((1, depth), f32), lefts, rights),
        in_specs=[SMEM] + [VMEM] * 2 + [ANY] * 2,
        out_specs=(VMEM,) * 5,
        scratch_shapes=[
            pltpu.VMEM((2, width, depth), bf16),
            pltpu.VMEM((2, depth, width), bf16),
            pltpu.VMEM((rows, width), f32),
            pltpu.VMEM((MAXSTEP * STAGES, rows, depth), f32),
            pltpu.VMEM((rows, width), f32),
            pltpu.SemaphoreType.DMA((2,)),
        ],
        compiler_params=pltpu.CompilerParams(vmem_limit_bytes=32 * 1024 * 1024),
        name="integrate",
    )(info, given, bias_in, own_w, other_w)


def level_of(peak):
    return jnp.ceil(256.0 * jnp.log2(jnp.maximum(peak, 1e-30))) + 1.0


def scale_of(level):
    return jnp.exp2(level * (1.0 / 256.0) - 15.0)


def steps_of(level):
    return jnp.exp2(15.0 - level * (1.0 / 256.0))


def whole(values):
    return jnp.round(values).astype(jnp.int32).astype(jnp.int16)


def head_of(bias):
    level = level_of(jnp.abs(bias))
    steps = bias * steps_of(level)
    high = jnp.round(steps)
    return level, high, (steps - high) * TOP


def code_piece(low, high, head, store, store_head):
    shared = len(low)
    row = lax.broadcasted_iota(jnp.int32, (HEAD, LANES), 0)
    tile = jnp.zeros((HEAD, LANES), f32)
    for at, values in enumerate(head):
        tile = jnp.where(row == shared + at, values, tile)
    for block in range(shared):
        pair = (low[block](), high[block]())
        peak = jnp.maximum(jnp.abs(pair[0]), jnp.abs(pair[1]))
        level = level_of(jnp.max(peak, axis=0, keepdims=True))
        steps = steps_of(level)
        tile = jnp.where(row == block, level, tile)
        store(block, whole(pair[0] * steps))
        store(block + shared, whole(pair[1] * steps))
    store_head(whole(tile))


def code_kernel(batches, keep_low, keep_high, got_low, got_high, bias, message):
    turns = bias.shape[1] // LANES
    owners = batches // turns
    depth = keep_low.shape[0] // turns
    piece = depth // owners
    shared = keep_low.shape[1] // LANES

    def turn(i, carry):
        rows = pl.ds(pl.multiple_of(i * depth, depth), depth)
        stretch = bias[:, pl.ds(pl.multiple_of(i * LANES, LANES), LANES)]

        def sums(kept, got):
            return [
                functools.partial(lambda c: kept[rows, c] + got[rows, c], pl.ds(at * LANES, LANES))
                for at in range(shared)
            ]

        def store(block, numbers):
            for owner in range(owners):
                message[i * owners + owner, pl.ds(block * piece, piece), :] = numbers[
                    owner * piece : (owner + 1) * piece
                ]

        def store_head(numbers):
            for owner in range(owners):
                message[i * owners + owner, pl.ds(2 * shared * piece, HEAD), :] = numbers

        code_piece(
            sums(keep_low, got_low), sums(keep_high, got_high), head_of(stretch), store, store_head
        )
        return carry

    lax.fori_loop(0, turns, turn, 0)


def code(keep, received, bias, batches):
    depth, middle = keep[0].shape
    height = depth // batches * (2 * middle // LANES) + HEAD
    return pl.pallas_call(
        functools.partial(code_kernel, batches),
        out_shape=jax.ShapeDtypeStruct((batches, height, LANES), jnp.int16),
        in_specs=[VMEM] * 5,
        out_specs=VMEM,
        compiler_params=pltpu.CompilerParams(vmem_limit_bytes=16 * 1024 * 1024),
        name="code",
    )(*keep, *received, bias)


def read_piece(blocks, load):
    piece = blocks[0][1]
    shared = len(blocks) // 2
    head = load(len(blocks) * piece, HEAD).astype(jnp.int32).astype(f32)
    scale = scale_of(head)
    high, low = head[shared + 1 : shared + 2], head[shared + 2 : shared + 3]
    bias = (high + low * (1.0 / TOP)) * scale[shared : shared + 1]
    values = []
    for block, (at, rows) in enumerate(blocks):
        share = block % shared
        numbers = load(at, rows).astype(jnp.int32).astype(f32)
        values.append(numbers * scale[share : share + 1])
    return values, bias


def blocks_of(height, count):
    piece = (height - HEAD) // count
    return [(block * piece, piece) for block in range(count)]


def decode_kernel(count, message, out):
    senders, height, _ = message.shape
    blocks = blocks_of(height, count)
    group = 4

    def turn(i, carry):
        bias, *sums = carry
        for j in range(group):
            values, more = read_piece(
                blocks, lambda at, rows: message[i * group + j, pl.ds(at, rows), :]
            )
            bias = bias + more
            sums = [one + other for one, other in zip(sums, values)]
        return (bias, *sums)

    zeros = (jnp.zeros((1, LANES), f32),) + (jnp.zeros((blocks[0][1], LANES), f32),) * count
    bias, *sums = lax.fori_loop(0, senders // group, turn, zeros)
    ready = [functools.partial(lambda v: v, value) for value in sums]

    def store(block, numbers):
        at, rows = blocks[block]
        out[pl.ds(at, rows), :] = numbers

    def store_head(numbers):
        out[pl.ds(height - HEAD, HEAD), :] = numbers

    code_piece(ready[: count // 2], ready[count // 2 :], head_of(bias), store, store_head)


def decode(message, count):
    return pl.pallas_call(
        functools.partial(decode_kernel, count),
        out_shape=jax.ShapeDtypeStruct(message.shape[1:], jnp.int16),
        in_specs=[VMEM],
        out_specs=VMEM,
        compiler_params=pltpu.CompilerParams(vmem_limit_bytes=8 * 1024 * 1024),
        name="decode",
    )(message)


def lay_out_kernel(scale, info, mine, by_core, by_zlo, by_both, grad_in, grad_out, grad_bias):
    core, offset = info[0], info[1]
    count = grad_in.shape[1] // LANES
    blocks = blocks_of(mine.shape[0], count)
    parts = []
    stretches = []
    for ref in (mine, by_core, by_zlo, by_both):
        values, bias = read_piece(
            blocks, functools.partial(lambda r, at, rows: r[pl.ds(at, rows), :], ref)
        )
        parts.append(values)
        stretches.append(bias)

    def fill(kept, other):
        for block in range(count):
            columns = pl.ds(block * LANES, LANES)
            kept[:, columns] = (parts[0][block] + parts[2][block]) * scale
            other[:, columns] = (parts[1][block] + parts[3][block]) * scale

    @pl.when(core == 0)
    def _():
        fill(grad_in, grad_out)

    @pl.when(core == 1)
    def _():
        fill(grad_out, grad_in)

    stretch = ((stretches[0] + stretches[3]) + (stretches[1] + stretches[2])) * scale
    turned = pltpu.roll(jnp.broadcast_to(stretch, (8, LANES)), LANES - offset, 1)
    grad_bias[...] = turned[0:1, : grad_bias.shape[1]]


def lay_out(scale, info, quarters, rows, width):
    gradient = jax.ShapeDtypeStruct((rows, width), f32)
    return pl.pallas_call(
        functools.partial(lay_out_kernel, scale),
        out_shape=(gradient, gradient, jax.ShapeDtypeStruct((1, rows), f32)),
        in_specs=[SMEM] + [VMEM] * 4,
        out_specs=(VMEM,) * 3,
        compiler_params=pltpu.CompilerParams(vmem_limit_bytes=8 * 1024 * 1024),
        name="lay_out",
    )(info, *quarters)


def contract_rows(left, right):
    return lax.dot_general(left, right, (((0,), (0,)), ((), ())), preferred_element_type=f32)


def shift_seg(block, distance):
    count = lax.axis_size(SEG)
    route = [(i - distance, i) for i in range(count) if 0 <= i - distance < count]
    return lax.ppermute(block, SEG, route)


def swap(block):
    return lax.ppermute(block, "core", [(0, 1), (1, 0)])


def body(starts, targets, counts, w_in, b_in, w_out):
    start = starts[0]
    core = lax.axis_index("core")
    place = lax.axis_index(SEG)
    batches = lax.axis_size("batch")
    rows, width = start.shape
    own = w_in.shape[0]

    following = shift_seg(start, -1)
    shard = jnp.where(core == 0, w_in, w_out)
    copies = jnp.broadcast_to(shard[None], (batches, own, width))
    own_w = lax.all_to_all(copies, "batch", 0, 0)
    own_w = own_w.reshape(batches * own, width)
    other_w = swap(own_w)
    given = jnp.stack([start, targets[0], following])

    has_next = (place < lax.axis_size(SEG) - 1).astype(jnp.int32)
    info = jnp.stack([counts[0], core, has_next])
    ends, bar, bias, left, right = integrate(info, given, b_in[None], own_w, other_w)
    previous = shift_seg(ends, 1)
    has_prev = (place > 0).astype(f32)
    grad_starts = (bar - penalty * ((previous - start) * has_prev))[None]

    received, keep = [], []
    for half in range(2):
        sent = contract_rows(left[0], right[0, half])
        received.append(swap(sent))
    for half in range(2):
        keep.append(contract_rows(left[1], right[1, half]))
    message = code(keep, received, bias, batches)
    message = lax.all_to_all(message, "batch", 0, 0)
    mine = decode(message, width // LANES)
    quarters = [mine] + [
        lax.ppermute(mine, SEG, [(i, i ^ flip) for i in range(4)]) for flip in (1, 2, 3)
    ]
    offset = lax.axis_index("batch") % (LANES // own) * own
    scale = 1.0 / math.sqrt(rows * batches)
    grad_in, grad_out, grad_bias = lay_out(scale, jnp.stack([core, offset]), quarters, own, width)
    return (grad_starts, grad_in, grad_out, grad_bias[0])


def solution(mesh):
    segs, batches = mesh.devices.shape
    finer = Mesh(mesh.devices.reshape(2, segs // 2, batches), ("zlo", "core", "batch"))
    return jax.shard_map(
        body,
        mesh=finer,
        in_specs=(
            P(SEG, "batch", None),
            P(SEG, "batch", None),
            P(SEG),
            P("batch", None),
            P(),
            P("batch", None),
        ),
        out_specs=(P(SEG, "batch", None), P("batch", None), P("batch", None), P("batch")),
        check_vma=False,
    )
```

```python
import functools
import math

import jax
import jax.numpy as jnp
from jax import lax
from jax.experimental import pallas as pl
from jax.experimental.pallas import tpu as pltpu
from jax.sharding import Mesh, PartitionSpec as P


MAXSTEP = 3
STAGES = 4
step_size = 0.25
penalty = 1.0
SEG = ("zlo", "core")
f32 = jnp.float32
bf16 = jnp.bfloat16
LANES = 128
HEAD = 8
TOP = 32767.0
VMEM = pl.BlockSpec(memory_space=pltpu.VMEM)
ANY = pl.BlockSpec(memory_space=pl.ANY)
SMEM = pl.BlockSpec(memory_space=pltpu.SMEM)


def product(left, right):
    return jnp.dot(left, right, preferred_element_type=f32)


def forward_kernel(
    info, given, bias_in, own_w, other_w,
    ends, left, w_turned, tanhs,
    w, state, total, sems,
):
    count, core = info[0], info[1]
    slot_in = 1 - core
    slot_out = core
    rows = state.shape[0]
    first = pltpu.make_async_copy(own_w, w.at[core], sems.at[0])
    second = pltpu.make_async_copy(other_w, w.at[1 - core], sems.at[1])
    first.start()
    second.start()
    state[...] = given[0]
    offset = bias_in[...]
    first.wait()
    second.wait()

    def place(at):
        return pl.ds(pl.multiple_of(at * rows, rows), rows)

    def field(u, at):
        inputs = u.astype(bf16)
        left[slot_in, place(at), :] = inputs
        hidden = jnp.tanh(product(inputs, w[0]) + offset)
        tanhs[at] = hidden
        low = hidden.astype(bf16)
        left[slot_out, place(at), :] = low
        return product(low, w[1])

    def turn(part):
        quarter = w.shape[1] // STAGES
        for which in range(2):
            rows_now = pl.ds(part * quarter, quarter)
            w_turned[which, :, rows_now] = w[which, rows_now, :].T

    def step(s, carry, beside=lambda part: None):
        at = STAGES * s
        beside(0)
        k = field(state[...], at)
        total[...] = k
        beside(1)
        k = field(state[...] + 0.5 * step_size * k, at + 1)
        total[...] += 2.0 * k
        beside(2)
        k = field(state[...] + 0.5 * step_size * k, at + 2)
        total[...] += 2.0 * k
        beside(3)
        k = field(state[...] + step_size * k, at + 3)
        state[...] = state[...] + step_size / 6.0 * (total[...] + k)
        return carry

    step(0, 0, turn)
    lax.fori_loop(1, count, step, 0)
    ends[...] = state[...]

    def clear(s, carry):
        block = pl.ds(pl.multiple_of(s * STAGES * rows, STAGES * rows), STAGES * rows)
        for slot in range(2):
            left[slot, block, :] = jnp.zeros((STAGES * rows, left.shape[2]), bf16)
        return carry

    lax.fori_loop(count, MAXSTEP, clear, 0)


def backward_kernel(
    info, given, following, ends, w_turned, tanhs, bar, bias, right, state, total, after, sem
):
    count, core, has_next = info[0], info[1], info[2].astype(f32)
    slot_in = 1 - core
    slot_out = core
    rows = state.shape[0]
    middle = right.shape[3]
    arrive = pltpu.make_async_copy(following, after, sem)
    arrive.start()
    bias[...] = jnp.zeros_like(bias)
    end = ends[...]
    arrive.wait()
    state[...] = (end - given[1]) + penalty * ((end - after[...]) * has_next)

    def place(at):
        return pl.ds(pl.multiple_of(at * rows, rows), rows)

    def field_back(q, at):
        outer = q.astype(bf16)
        right[slot_out, 0, place(at), :] = outer[:, :middle]
        right[slot_out, 1, place(at), :] = outer[:, middle:]
        hidden = tanhs[at]
        inner = product(outer, w_turned[1]) * (1.0 - hidden * hidden)
        bias[...] += jnp.sum(inner, axis=0, keepdims=True)
        low = inner.astype(bf16)
        right[slot_in, 0, place(at), :] = low[:, :middle]
        right[slot_in, 1, place(at), :] = low[:, middle:]
        return product(low, w_turned[0])

    def step(turn, carry):
        at = STAGES * (count - 1 - turn)
        g = field_back(step_size / 6.0 * state[...], at + 3)
        total[...] = state[...] + g
        g = field_back(step_size / 3.0 * state[...] + step_size * g, at + 2)
        total[...] += g
        g = field_back(step_size / 3.0 * state[...] + 0.5 * step_size * g, at + 1)
        total[...] += g
        g = field_back(step_size / 6.0 * state[...] + 0.5 * step_size * g, at)
        state[...] = total[...] + g
        return carry

    lax.fori_loop(0, count, step, 0)
    bar[...] = state[...]

    def clear(s, carry):
        block = pl.ds(pl.multiple_of(s * STAGES * rows, STAGES * rows), STAGES * rows)
        for slot in range(2):
            for half in range(2):
                right[slot, half, block, :] = jnp.zeros((STAGES * rows, middle), bf16)
        return carry

    lax.fori_loop(count, MAXSTEP, clear, 0)


def forward(info, given, bias_in, own_w, other_w):
    _, rows, width = given.shape
    depth = own_w.shape[1]
    terms = MAXSTEP * STAGES * rows
    return pl.pallas_call(
        forward_kernel,
        out_shape=(
            jax.ShapeDtypeStruct((rows, width), f32),
            jax.ShapeDtypeStruct((2, terms, width), bf16),
            jax.ShapeDtypeStruct((2, depth, width), bf16),
            jax.ShapeDtypeStruct((MAXSTEP * STAGES, rows, depth), f32),
        ),
        in_specs=[SMEM] + [VMEM] * 2 + [ANY] * 2,
        out_specs=(VMEM,) * 4,
        scratch_shapes=[
            pltpu.VMEM((2, width, depth), bf16),
            pltpu.VMEM((rows, width), f32),
            pltpu.VMEM((rows, width), f32),
            pltpu.SemaphoreType.DMA((2,)),
        ],
        compiler_params=pltpu.CompilerParams(vmem_limit_bytes=26 * 1024 * 1024),
        name="forward",
    )(info, given, bias_in, own_w, other_w)


def backward(info, given, following, ends, w_turned, tanhs):
    rows, width = ends.shape
    depth = w_turned.shape[1]
    return pl.pallas_call(
        backward_kernel,
        out_shape=(
            jax.ShapeDtypeStruct((rows, width), f32),
            jax.ShapeDtypeStruct((1, depth), f32),
            jax.ShapeDtypeStruct((2, 2, MAXSTEP * STAGES * rows, width // 2), bf16),
        ),
        in_specs=[SMEM, VMEM, ANY] + [VMEM] * 3,
        out_specs=(VMEM,) * 3,
        scratch_shapes=[pltpu.VMEM((rows, width), f32)] * 3 + [pltpu.SemaphoreType.DMA],
        compiler_params=pltpu.CompilerParams(vmem_limit_bytes=22 * 1024 * 1024),
        name="backward",
    )(info, given, following, ends, w_turned, tanhs)


def level_of(peak):
    return jnp.ceil(256.0 * jnp.log2(jnp.maximum(peak, 1e-30))) + 1.0


def scale_of(level):
    return jnp.exp2(level * (1.0 / 256.0) - 15.0)


def steps_of(level):
    return jnp.exp2(15.0 - level * (1.0 / 256.0))


def whole(values):
    return jnp.round(values).astype(jnp.int32).astype(jnp.int16)


def head_of(bias):
    level = level_of(jnp.abs(bias))
    steps = bias * steps_of(level)
    high = jnp.round(steps)
    return level, high, (steps - high) * TOP


def code_piece(low, high, head, store, store_head):
    shared = len(low)
    row = lax.broadcasted_iota(jnp.int32, (HEAD, LANES), 0)
    tile = jnp.zeros((HEAD, LANES), f32)
    for at, values in enumerate(head):
        tile = jnp.where(row == shared + at, values, tile)
    for block in range(shared):
        pair = (low[block](), high[block]())
        peak = jnp.maximum(jnp.abs(pair[0]), jnp.abs(pair[1]))
        level = level_of(jnp.max(peak, axis=0, keepdims=True))
        steps = steps_of(level)
        tile = jnp.where(row == block, level, tile)
        store(block, whole(pair[0] * steps))
        store(block + shared, whole(pair[1] * steps))
    store_head(whole(tile))


def code_kernel(batches, keep_low, keep_high, got_low, got_high, bias, message):
    turns = bias.shape[1] // LANES
    owners = batches // turns
    depth = keep_low.shape[0] // turns
    piece = depth // owners
    shared = keep_low.shape[1] // LANES

    def turn(i, carry):
        rows = pl.ds(pl.multiple_of(i * depth, depth), depth)
        stretch = bias[:, pl.ds(pl.multiple_of(i * LANES, LANES), LANES)]

        def sums(kept, got):
            return [
                functools.partial(lambda c: kept[rows, c] + got[rows, c], pl.ds(at * LANES, LANES))
                for at in range(shared)
            ]

        def store(block, numbers):
            for owner in range(owners):
                message[i * owners + owner, pl.ds(block * piece, piece), :] = numbers[
                    owner * piece : (owner + 1) * piece
                ]

        def store_head(numbers):
            for owner in range(owners):
                message[i * owners + owner, pl.ds(2 * shared * piece, HEAD), :] = numbers

        code_piece(
            sums(keep_low, got_low), sums(keep_high, got_high), head_of(stretch), store, store_head
        )
        return carry

    lax.fori_loop(0, turns, turn, 0)


def code(keep, received, bias, batches):
    depth, middle = keep[0].shape
    height = depth // batches * (2 * middle // LANES) + HEAD
    return pl.pallas_call(
        functools.partial(code_kernel, batches),
        out_shape=jax.ShapeDtypeStruct((batches, height, LANES), jnp.int16),
        in_specs=[VMEM] * 5,
        out_specs=VMEM,
        compiler_params=pltpu.CompilerParams(vmem_limit_bytes=16 * 1024 * 1024),
        name="code",
    )(*keep, *received, bias)


def read_piece(blocks, load):
    piece = blocks[0][1]
    shared = len(blocks) // 2
    head = load(len(blocks) * piece, HEAD).astype(jnp.int32).astype(f32)
    scale = scale_of(head)
    high, low = head[shared + 1 : shared + 2], head[shared + 2 : shared + 3]
    bias = (high + low * (1.0 / TOP)) * scale[shared : shared + 1]
    values = []
    for block, (at, rows) in enumerate(blocks):
        share = block % shared
        numbers = load(at, rows).astype(jnp.int32).astype(f32)
        values.append(numbers * scale[share : share + 1])
    return values, bias


def blocks_of(height, count):
    piece = (height - HEAD) // count
    return [(block * piece, piece) for block in range(count)]


def decode_kernel(count, message, out):
    senders, height, _ = message.shape
    blocks = blocks_of(height, count)
    group = 4

    def turn(i, carry):
        bias, *sums = carry
        for j in range(group):
            values, more = read_piece(
                blocks, lambda at, rows: message[i * group + j, pl.ds(at, rows), :]
            )
            bias = bias + more
            sums = [one + other for one, other in zip(sums, values)]
        return (bias, *sums)

    zeros = (jnp.zeros((1, LANES), f32),) + (jnp.zeros((blocks[0][1], LANES), f32),) * count
    bias, *sums = lax.fori_loop(0, senders // group, turn, zeros)
    ready = [functools.partial(lambda v: v, value) for value in sums]

    def store(block, numbers):
        at, rows = blocks[block]
        out[pl.ds(at, rows), :] = numbers

    def store_head(numbers):
        out[pl.ds(height - HEAD, HEAD), :] = numbers

    code_piece(ready[: count // 2], ready[count // 2 :], head_of(bias), store, store_head)


def decode(message, count):
    return pl.pallas_call(
        functools.partial(decode_kernel, count),
        out_shape=jax.ShapeDtypeStruct(message.shape[1:], jnp.int16),
        in_specs=[VMEM],
        out_specs=VMEM,
        compiler_params=pltpu.CompilerParams(vmem_limit_bytes=8 * 1024 * 1024),
        name="decode",
    )(message)


def lay_out_kernel(scale, info, mine, by_core, by_zlo, by_both, grad_in, grad_out, grad_bias):
    core, offset = info[0], info[1]
    count = grad_in.shape[1] // LANES
    blocks = blocks_of(mine.shape[0], count)
    parts = []
    stretches = []
    for ref in (mine, by_core, by_zlo, by_both):
        values, bias = read_piece(
            blocks, functools.partial(lambda r, at, rows: r[pl.ds(at, rows), :], ref)
        )
        parts.append(values)
        stretches.append(bias)

    def fill(kept, other):
        for block in range(count):
            columns = pl.ds(block * LANES, LANES)
            kept[:, columns] = (parts[0][block] + parts[2][block]) * scale
            other[:, columns] = (parts[1][block] + parts[3][block]) * scale

    @pl.when(core == 0)
    def _():
        fill(grad_in, grad_out)

    @pl.when(core == 1)
    def _():
        fill(grad_out, grad_in)

    stretch = ((stretches[0] + stretches[3]) + (stretches[1] + stretches[2])) * scale
    turned = pltpu.roll(jnp.broadcast_to(stretch, (8, LANES)), LANES - offset, 1)
    grad_bias[...] = turned[0:1, : grad_bias.shape[1]]


def lay_out(scale, info, quarters, rows, width):
    gradient = jax.ShapeDtypeStruct((rows, width), f32)
    return pl.pallas_call(
        functools.partial(lay_out_kernel, scale),
        out_shape=(gradient, gradient, jax.ShapeDtypeStruct((1, rows), f32)),
        in_specs=[SMEM] + [VMEM] * 4,
        out_specs=(VMEM,) * 3,
        compiler_params=pltpu.CompilerParams(vmem_limit_bytes=8 * 1024 * 1024),
        name="lay_out",
    )(info, *quarters)


def contract_rows(left, right):
    return lax.dot_general(left, right, (((0,), (0,)), ((), ())), preferred_element_type=f32)


def shift_seg(block, distance):
    count = lax.axis_size(SEG)
    route = [(i - distance, i) for i in range(count) if 0 <= i - distance < count]
    return lax.ppermute(block, SEG, route)


def swap(block):
    return lax.ppermute(block, "core", [(0, 1), (1, 0)])


def body(starts, targets, counts, w_in, b_in, w_out):
    start = starts[0]
    core = lax.axis_index("core")
    place = lax.axis_index(SEG)
    batches = lax.axis_size("batch")
    rows, width = start.shape
    own = w_in.shape[0]

    following = shift_seg(start, -1)
    shard = jnp.where(core == 0, w_in, w_out)
    copies = jnp.broadcast_to(shard[None], (batches, own, width))
    own_w = lax.all_to_all(copies, "batch", 0, 0)
    own_w = own_w.reshape(batches * own, width)
    other_w = swap(own_w)
    given = jnp.stack([start, targets[0]])

    has_next = (place < lax.axis_size(SEG) - 1).astype(jnp.int32)
    info = jnp.stack([counts[0], core, has_next])
    ends, left, w_turned, tanhs = forward(info, given, b_in[None], own_w, other_w)
    bar, bias, right = backward(info, given, pltpu.with_memory_space_constraint(following, pltpu.HBM), ends, w_turned, tanhs)
    previous = shift_seg(ends, 1)
    has_prev = (place > 0).astype(f32)
    grad_starts = (bar - penalty * ((previous - start) * has_prev))[None]

    received, keep = [], []
    for half in range(2):
        sent = contract_rows(left[0], right[0, half])
        received.append(swap(sent))
    for half in range(2):
        keep.append(contract_rows(left[1], right[1, half]))
    message = code(keep, received, bias, batches)
    message = lax.all_to_all(message, "batch", 0, 0)
    mine = decode(message, width // LANES)
    quarters = [mine] + [
        lax.ppermute(mine, SEG, [(i, i ^ flip) for i in range(4)]) for flip in (1, 2, 3)
    ]
    offset = lax.axis_index("batch") % (LANES // own) * own
    scale = 1.0 / math.sqrt(rows * batches)
    grad_in, grad_out, grad_bias = lay_out(scale, jnp.stack([core, offset]), quarters, own, width)
    return (grad_starts, grad_in, grad_out, grad_bias[0])


def solution(mesh):
    segs, batches = mesh.devices.shape
    finer = Mesh(mesh.devices.reshape(2, segs // 2, batches), ("zlo", "core", "batch"))
    return jax.shard_map(
        body,
        mesh=finer,
        in_specs=(
            P(SEG, "batch", None),
            P(SEG, "batch", None),
            P(SEG),
            P("batch", None),
            P(),
            P("batch", None),
        ),
        out_specs=(P(SEG, "batch", None), P("batch", None), P("batch", None), P("batch")),
        check_vma=False,
    )
```

```python
import functools
import math

import jax
import jax.numpy as jnp
from jax import lax
from jax.experimental import pallas as pl
from jax.experimental.pallas import tpu as pltpu
from jax.sharding import Mesh, PartitionSpec as P


MAXSTEP = 3
STAGES = 4
step_size = 0.25
penalty = 1.0
SEG = ("zlo", "core")
f32 = jnp.float32
bf16 = jnp.bfloat16
LANES = 128
HEAD = 8
TOP = 32767.0
VMEM = pl.BlockSpec(memory_space=pltpu.VMEM)
ANY = pl.BlockSpec(memory_space=pl.ANY)
SMEM = pl.BlockSpec(memory_space=pltpu.SMEM)


def packed_options(mebibytes):
    return pltpu.CompilerParams(vmem_limit_bytes=mebibytes * 1024 * 1024)


def product(left, right):
    return jnp.dot(left, right, preferred_element_type=f32)


def forward_kernel(
    info, given, bias_in, own_w, other_w,
    ends, left, w_turned, tanhs,
    w, state, total, sems,
):
    count, core = info[0], info[1]
    slot_in = 1 - core
    slot_out = core
    rows = state.shape[0]
    first = pltpu.make_async_copy(own_w, w.at[core], sems.at[0])
    second = pltpu.make_async_copy(other_w, w.at[1 - core], sems.at[1])
    first.start()
    second.start()
    state[...] = given[0]
    offset = bias_in[...]
    first.wait()
    second.wait()

    def place(at):
        return pl.ds(pl.multiple_of(at * rows, rows), rows)

    def field(u, at):
        inputs = u.astype(bf16)
        left[slot_in, place(at), :] = inputs
        hidden = jnp.tanh(product(inputs, w[0]) + offset)
        tanhs[at] = hidden
        low = hidden.astype(bf16)
        left[slot_out, place(at), :] = low
        return product(low, w[1])

    def turn(part):
        quarter = w.shape[1] // STAGES
        for which in range(2):
            rows_now = pl.ds(part * quarter, quarter)
            w_turned[which, :, rows_now] = w[which, rows_now, :].T

    def step(s, carry, beside=lambda part: None):
        at = STAGES * s
        beside(0)
        k = field(state[...], at)
        total[...] = k
        beside(1)
        k = field(state[...] + 0.5 * step_size * k, at + 1)
        total[...] += 2.0 * k
        beside(2)
        k = field(state[...] + 0.5 * step_size * k, at + 2)
        total[...] += 2.0 * k
        beside(3)
        k = field(state[...] + step_size * k, at + 3)
        state[...] = state[...] + step_size / 6.0 * (total[...] + k)
        return carry

    step(0, 0, turn)
    lax.fori_loop(1, count, step, 0)
    ends[...] = state[...]

    def clear(s, carry):
        block = pl.ds(pl.multiple_of(s * STAGES * rows, STAGES * rows), STAGES * rows)
        for slot in range(2):
            left[slot, block, :] = jnp.zeros((STAGES * rows, left.shape[2]), bf16)
        return carry

    lax.fori_loop(count, MAXSTEP, clear, 0)


def backward_kernel(
    info, given, following, ends, w_turned, tanhs, bar, bias, right, state, total, after, sem
):
    count, core, has_next = info[0], info[1], info[2].astype(f32)
    slot_in = 1 - core
    slot_out = core
    rows = state.shape[0]
    middle = right.shape[3]
    arrive = pltpu.make_async_copy(following, after, sem)
    arrive.start()
    bias[...] = jnp.zeros_like(bias)
    end = ends[...]
    arrive.wait()
    state[...] = (end - given[1]) + penalty * ((end - after[...]) * has_next)

    def place(at):
        return pl.ds(pl.multiple_of(at * rows, rows), rows)

    def field_back(q, at):
        outer = q.astype(bf16)
        right[slot_out, 0, place(at), :] = outer[:, :middle]
        right[slot_out, 1, place(at), :] = outer[:, middle:]
        hidden = tanhs[at]
        inner = product(outer, w_turned[1]) * (1.0 - hidden * hidden)
        bias[...] += jnp.sum(inner, axis=0, keepdims=True)
        low = inner.astype(bf16)
        right[slot_in, 0, place(at), :] = low[:, :middle]
        right[slot_in, 1, place(at), :] = low[:, middle:]
        return product(low, w_turned[0])

    def step(turn, carry):
        at = STAGES * (count - 1 - turn)
        g = field_back(step_size / 6.0 * state[...], at + 3)
        total[...] = state[...] + g
        g = field_back(step_size / 3.0 * state[...] + step_size * g, at + 2)
        total[...] += g
        g = field_back(step_size / 3.0 * state[...] + 0.5 * step_size * g, at + 1)
        total[...] += g
        g = field_back(step_size / 6.0 * state[...] + 0.5 * step_size * g, at)
        state[...] = total[...] + g
        return carry

    lax.fori_loop(0, count, step, 0)
    bar[...] = state[...]

    def clear(s, carry):
        block = pl.ds(pl.multiple_of(s * STAGES * rows, STAGES * rows), STAGES * rows)
        for slot in range(2):
            for half in range(2):
                right[slot, half, block, :] = jnp.zeros((STAGES * rows, middle), bf16)
        return carry

    lax.fori_loop(count, MAXSTEP, clear, 0)


def forward(info, given, bias_in, own_w, other_w):
    _, rows, width = given.shape
    depth = own_w.shape[1]
    terms = MAXSTEP * STAGES * rows
    return pl.pallas_call(
        forward_kernel,
        out_shape=(
            jax.ShapeDtypeStruct((rows, width), f32),
            jax.ShapeDtypeStruct((2, terms, width), bf16),
            jax.ShapeDtypeStruct((2, depth, width), bf16),
            jax.ShapeDtypeStruct((MAXSTEP * STAGES, rows, depth), f32),
        ),
        in_specs=[SMEM] + [VMEM] * 2 + [ANY] * 2,
        out_specs=(VMEM,) * 4,
        scratch_shapes=[
            pltpu.VMEM((2, width, depth), bf16),
            pltpu.VMEM((rows, width), f32),
            pltpu.VMEM((rows, width), f32),
            pltpu.SemaphoreType.DMA((2,)),
        ],
        compiler_params=packed_options(26),
        name="forward",
    )(info, given, bias_in, own_w, other_w)


def backward(info, given, following, ends, w_turned, tanhs):
    rows, width = ends.shape
    depth = w_turned.shape[1]
    return pl.pallas_call(
        backward_kernel,
        out_shape=(
            jax.ShapeDtypeStruct((rows, width), f32),
            jax.ShapeDtypeStruct((1, depth), f32),
            jax.ShapeDtypeStruct((2, 2, MAXSTEP * STAGES * rows, width // 2), bf16),
        ),
        in_specs=[SMEM, VMEM, ANY] + [VMEM] * 3,
        out_specs=(VMEM,) * 3,
        scratch_shapes=[pltpu.VMEM((rows, width), f32)] * 3 + [pltpu.SemaphoreType.DMA],
        compiler_params=packed_options(22),
        name="backward",
    )(info, given, following, ends, w_turned, tanhs)


def level_of(peak):
    return jnp.ceil(256.0 * jnp.log2(jnp.maximum(peak, 1e-30))) + 1.0


def scale_of(level):
    return jnp.exp2(level * (1.0 / 256.0) - 15.0)


def steps_of(level):
    return jnp.exp2(15.0 - level * (1.0 / 256.0))


def whole(values):
    return jnp.round(values).astype(jnp.int32).astype(jnp.int16)


def head_of(bias):
    level = level_of(jnp.abs(bias))
    steps = bias * steps_of(level)
    high = jnp.round(steps)
    return level, high, (steps - high) * TOP


def code_piece(low, high, head, store, store_head):
    shared = len(low)
    row = lax.broadcasted_iota(jnp.int32, (HEAD, LANES), 0)
    tile = jnp.zeros((HEAD, LANES), f32)
    for at, values in enumerate(head):
        tile = jnp.where(row == shared + at, values, tile)
    for block in range(shared):
        pair = (low[block](), high[block]())
        peak = jnp.maximum(jnp.abs(pair[0]), jnp.abs(pair[1]))
        level = level_of(jnp.max(peak, axis=0, keepdims=True))
        steps = steps_of(level)
        tile = jnp.where(row == block, level, tile)
        store(block, whole(pair[0] * steps))
        store(block + shared, whole(pair[1] * steps))
    store_head(whole(tile))


def code_kernel(batches, keep_low, keep_high, got_low, got_high, bias, message):
    turns = bias.shape[1] // LANES
    owners = batches // turns
    depth = keep_low.shape[0] // turns
    piece = depth // owners
    shared = keep_low.shape[1] // LANES

    def turn(i, carry):
        rows = pl.ds(pl.multiple_of(i * depth, depth), depth)
        stretch = bias[:, pl.ds(pl.multiple_of(i * LANES, LANES), LANES)]

        def sums(kept, got):
            return [
                functools.partial(lambda c: kept[rows, c] + got[rows, c], pl.ds(at * LANES, LANES))
                for at in range(shared)
            ]

        def store(block, numbers):
            for owner in range(owners):
                message[i * owners + owner, pl.ds(block * piece, piece), :] = numbers[
                    owner * piece : (owner + 1) * piece
                ]

        def store_head(numbers):
            for owner in range(owners):
                message[i * owners + owner, pl.ds(2 * shared * piece, HEAD), :] = numbers

        code_piece(
            sums(keep_low, got_low), sums(keep_high, got_high), head_of(stretch), store, store_head
        )
        return carry

    lax.fori_loop(0, turns, turn, 0)


def code(keep, received, bias, batches):
    depth, middle = keep[0].shape
    height = depth // batches * (2 * middle // LANES) + HEAD
    return pl.pallas_call(
        functools.partial(code_kernel, batches),
        out_shape=jax.ShapeDtypeStruct((batches, height, LANES), jnp.int16),
        in_specs=[VMEM] * 5,
        out_specs=VMEM,
        compiler_params=pltpu.CompilerParams(vmem_limit_bytes=16 * 1024 * 1024),
        name="code",
    )(*keep, *received, bias)


def read_piece(blocks, load):
    piece = blocks[0][1]
    shared = len(blocks) // 2
    head = load(len(blocks) * piece, HEAD).astype(jnp.int32).astype(f32)
    scale = scale_of(head)
    high, low = head[shared + 1 : shared + 2], head[shared + 2 : shared + 3]
    bias = (high + low * (1.0 / TOP)) * scale[shared : shared + 1]
    values = []
    for block, (at, rows) in enumerate(blocks):
        share = block % shared
        numbers = load(at, rows).astype(jnp.int32).astype(f32)
        values.append(numbers * scale[share : share + 1])
    return values, bias


def blocks_of(height, count):
    piece = (height - HEAD) // count
    return [(block * piece, piece) for block in range(count)]


def decode_kernel(count, message, out):
    senders, height, _ = message.shape
    blocks = blocks_of(height, count)
    group = 4

    def turn(i, carry):
        bias, *sums = carry
        for j in range(group):
            values, more = read_piece(
                blocks, lambda at, rows: message[i * group + j, pl.ds(at, rows), :]
            )
            bias = bias + more
            sums = [one + other for one, other in zip(sums, values)]
        return (bias, *sums)

    zeros = (jnp.zeros((1, LANES), f32),) + (jnp.zeros((blocks[0][1], LANES), f32),) * count
    bias, *sums = lax.fori_loop(0, senders // group, turn, zeros)
    ready = [functools.partial(lambda v: v, value) for value in sums]

    def store(block, numbers):
        at, rows = blocks[block]
        out[pl.ds(at, rows), :] = numbers

    def store_head(numbers):
        out[pl.ds(height - HEAD, HEAD), :] = numbers

    code_piece(ready[: count // 2], ready[count // 2 :], head_of(bias), store, store_head)


def decode(message, count):
    return pl.pallas_call(
        functools.partial(decode_kernel, count),
        out_shape=jax.ShapeDtypeStruct(message.shape[1:], jnp.int16),
        in_specs=[VMEM],
        out_specs=VMEM,
        compiler_params=pltpu.CompilerParams(vmem_limit_bytes=8 * 1024 * 1024),
        name="decode",
    )(message)


def lay_out_kernel(scale, info, mine, by_core, by_zlo, by_both, grad_in, grad_out, grad_bias):
    core, offset = info[0], info[1]
    count = grad_in.shape[1] // LANES
    blocks = blocks_of(mine.shape[0], count)
    parts = []
    stretches = []
    for ref in (mine, by_core, by_zlo, by_both):
        values, bias = read_piece(
            blocks, functools.partial(lambda r, at, rows: r[pl.ds(at, rows), :], ref)
        )
        parts.append(values)
        stretches.append(bias)

    def fill(kept, other):
        for block in range(count):
            columns = pl.ds(block * LANES, LANES)
            kept[:, columns] = (parts[0][block] + parts[2][block]) * scale
            other[:, columns] = (parts[1][block] + parts[3][block]) * scale

    @pl.when(core == 0)
    def _():
        fill(grad_in, grad_out)

    @pl.when(core == 1)
    def _():
        fill(grad_out, grad_in)

    stretch = ((stretches[0] + stretches[3]) + (stretches[1] + stretches[2])) * scale
    turned = pltpu.roll(jnp.broadcast_to(stretch, (8, LANES)), LANES - offset, 1)
    grad_bias[...] = turned[0:1, : grad_bias.shape[1]]


def lay_out(scale, info, quarters, rows, width):
    gradient = jax.ShapeDtypeStruct((rows, width), f32)
    return pl.pallas_call(
        functools.partial(lay_out_kernel, scale),
        out_shape=(gradient, gradient, jax.ShapeDtypeStruct((1, rows), f32)),
        in_specs=[SMEM] + [VMEM] * 4,
        out_specs=(VMEM,) * 3,
        compiler_params=pltpu.CompilerParams(vmem_limit_bytes=8 * 1024 * 1024),
        name="lay_out",
    )(info, *quarters)


def contract_rows(left, right):
    return lax.dot_general(left, right, (((0,), (0,)), ((), ())), preferred_element_type=f32)


def shift_seg(block, distance):
    count = lax.axis_size(SEG)
    route = [(i - distance, i) for i in range(count) if 0 <= i - distance < count]
    return lax.ppermute(block, SEG, route)


def swap(block):
    return lax.ppermute(block, "core", [(0, 1), (1, 0)])


def body(starts, targets, counts, w_in, b_in, w_out):
    start = starts[0]
    core = lax.axis_index("core")
    place = lax.axis_index(SEG)
    batches = lax.axis_size("batch")
    rows, width = start.shape
    own = w_in.shape[0]

    following = shift_seg(start, -1)
    shard = jnp.where(core == 0, w_in, w_out)
    copies = jnp.broadcast_to(shard[None], (batches, own, width))
    own_w = lax.all_to_all(copies, "batch", 0, 0)
    own_w = own_w.reshape(batches * own, width)
    other_w = swap(own_w)
    given = jnp.stack([start, targets[0]])

    has_next = (place < lax.axis_size(SEG) - 1).astype(jnp.int32)
    info = jnp.stack([counts[0], core, has_next])
    ends, left, w_turned, tanhs = forward(info, given, b_in[None], own_w, other_w)
    bar, bias, right = backward(info, given, pltpu.with_memory_space_constraint(following, pltpu.HBM), ends, w_turned, tanhs)
    previous = shift_seg(ends, 1)
    has_prev = (place > 0).astype(f32)
    grad_starts = (bar - penalty * ((previous - start) * has_prev))[None]

    received, keep = [], []
    for half in range(2):
        sent = contract_rows(left[0], right[0, half])
        received.append(swap(sent))
    for half in range(2):
        keep.append(contract_rows(left[1], right[1, half]))
    message = code(keep, received, bias, batches)
    message = lax.all_to_all(message, "batch", 0, 0)
    mine = decode(message, width // LANES)
    quarters = [mine] + [
        lax.ppermute(mine, SEG, [(i, i ^ flip) for i in range(4)]) for flip in (1, 2, 3)
    ]
    offset = lax.axis_index("batch") % (LANES // own) * own
    scale = 1.0 / math.sqrt(rows * batches)
    grad_in, grad_out, grad_bias = lay_out(scale, jnp.stack([core, offset]), quarters, own, width)
    return (grad_starts, grad_in, grad_out, grad_bias[0])


def solution(mesh):
    segs, batches = mesh.devices.shape
    finer = Mesh(mesh.devices.reshape(2, segs // 2, batches), ("zlo", "core", "batch"))
    return jax.shard_map(
        body,
        mesh=finer,
        in_specs=(
            P(SEG, "batch", None),
            P(SEG, "batch", None),
            P(SEG),
            P("batch", None),
            P(),
            P("batch", None),
        ),
        out_specs=(P(SEG, "batch", None), P("batch", None), P("batch", None), P("batch")),
        check_vma=False,
    )
```

```python
import functools
import math

import jax
import jax.numpy as jnp
from jax import lax
from jax.experimental import pallas as pl
from jax.experimental.pallas import tpu as pltpu
from jax.sharding import Mesh, PartitionSpec as P


MAXSTEP = 3
STAGES = 4
step_size = 0.25
penalty = 1.0
SEG = ("zlo", "core")
f32 = jnp.float32
bf16 = jnp.bfloat16
LANES = 128
HEAD = 8
TOP = 32767.0
VMEM = pl.BlockSpec(memory_space=pltpu.VMEM)
ANY = pl.BlockSpec(memory_space=pl.ANY)
SMEM = pl.BlockSpec(memory_space=pltpu.SMEM)


def packed_options(mebibytes):
    return pltpu.CompilerParams(vmem_limit_bytes=mebibytes * 1024 * 1024)


def product(left, right):
    return jnp.dot(left, right, preferred_element_type=f32)


def forward_kernel(
    info, given, bias_in, own_w, other_w,
    ends, left, w_turned, tanhs,
    w, state, total, sems,
):
    count, core = info[0], info[1]
    slot_in = 1 - core
    slot_out = core
    rows = state.shape[0]
    first = pltpu.make_async_copy(own_w, w.at[core], sems.at[0])
    second = pltpu.make_async_copy(other_w, w.at[1 - core], sems.at[1])
    first.start()
    second.start()
    state[...] = given[0]
    offset = bias_in[...]
    first.wait()
    second.wait()

    def place(at):
        return pl.ds(pl.multiple_of(at * rows, rows), rows)

    def field(u, at):
        inputs = u.astype(bf16)
        left[slot_in, place(at), :] = inputs
        hidden = jnp.tanh(product(inputs, w[0]) + offset)
        tanhs[at] = hidden
        low = hidden.astype(bf16)
        left[slot_out, place(at), :] = low
        return product(low, w[1])

    def turn(part):
        quarter = w.shape[1] // STAGES
        for which in range(2):
            rows_now = pl.ds(part * quarter, quarter)
            w_turned[which, :, rows_now] = w[which, rows_now, :].T

    def step(s, carry, beside=lambda part: None):
        at = STAGES * s
        beside(0)
        k = field(state[...], at)
        total[...] = k
        beside(1)
        k = field(state[...] + 0.5 * step_size * k, at + 1)
        total[...] += 2.0 * k
        beside(2)
        k = field(state[...] + 0.5 * step_size * k, at + 2)
        total[...] += 2.0 * k
        beside(3)
        k = field(state[...] + step_size * k, at + 3)
        state[...] = state[...] + step_size / 6.0 * (total[...] + k)
        return carry

    step(0, 0, turn)
    lax.fori_loop(1, count, step, 0)
    ends[...] = state[...]

    def clear(s, carry):
        block = pl.ds(pl.multiple_of(s * STAGES * rows, STAGES * rows), STAGES * rows)
        for slot in range(2):
            left[slot, block, :] = jnp.zeros((STAGES * rows, left.shape[2]), bf16)
        return carry

    lax.fori_loop(count, MAXSTEP, clear, 0)


def backward_kernel(
    info, given, following, ends, w_turned, tanhs, bar, bias, right, state, total, after, sem
):
    count, core, has_next = info[0], info[1], info[2].astype(f32)
    slot_in = 1 - core
    slot_out = core
    rows = state.shape[0]
    middle = right.shape[3]
    arrive = pltpu.make_async_copy(following, after, sem)
    arrive.start()
    bias[...] = jnp.zeros_like(bias)
    end = ends[...]
    arrive.wait()
    state[...] = (end - given[1]) + penalty * ((end - after[...]) * has_next)

    def place(at):
        return pl.ds(pl.multiple_of(at * rows, rows), rows)

    def field_back(q, at):
        outer = q.astype(bf16)
        right[slot_out, 0, place(at), :] = outer[:, :middle]
        right[slot_out, 1, place(at), :] = outer[:, middle:]
        hidden = tanhs[at]
        inner = product(outer, w_turned[1]) * (1.0 - hidden * hidden)
        bias[...] += jnp.sum(inner, axis=0, keepdims=True)
        low = inner.astype(bf16)
        right[slot_in, 0, place(at), :] = low[:, :middle]
        right[slot_in, 1, place(at), :] = low[:, middle:]
        return product(low, w_turned[0])

    def step(turn, carry):
        at = STAGES * (count - 1 - turn)
        g = field_back(step_size / 6.0 * state[...], at + 3)
        total[...] = state[...] + g
        g = field_back(step_size / 3.0 * state[...] + step_size * g, at + 2)
        total[...] += g
        g = field_back(step_size / 3.0 * state[...] + 0.5 * step_size * g, at + 1)
        total[...] += g
        g = field_back(step_size / 6.0 * state[...] + 0.5 * step_size * g, at)
        state[...] = total[...] + g
        return carry

    lax.fori_loop(0, count, step, 0)
    bar[...] = state[...]

    def clear(s, carry):
        block = pl.ds(pl.multiple_of(s * STAGES * rows, STAGES * rows), STAGES * rows)
        for slot in range(2):
            for half in range(2):
                right[slot, half, block, :] = jnp.zeros((STAGES * rows, middle), bf16)
        return carry

    lax.fori_loop(count, MAXSTEP, clear, 0)


def forward(info, given, bias_in, own_w, other_w):
    _, rows, width = given.shape
    depth = own_w.shape[1]
    terms = MAXSTEP * STAGES * rows
    return pl.pallas_call(
        forward_kernel,
        out_shape=(
            jax.ShapeDtypeStruct((rows, width), f32),
            jax.ShapeDtypeStruct((2, terms, width), bf16),
            jax.ShapeDtypeStruct((2, depth, width), bf16),
            jax.ShapeDtypeStruct((MAXSTEP * STAGES, rows, depth), f32),
        ),
        in_specs=[SMEM] + [VMEM] * 2 + [ANY] * 2,
        out_specs=(VMEM,) * 4,
        scratch_shapes=[
            pltpu.VMEM((2, width, depth), bf16),
            pltpu.VMEM((rows, width), f32),
            pltpu.VMEM((rows, width), f32),
            pltpu.SemaphoreType.DMA((2,)),
        ],
        compiler_params=packed_options(26),
        name="forward",
    )(info, given, bias_in, own_w, other_w)


def backward(info, given, following, ends, w_turned, tanhs):
    rows, width = ends.shape
    depth = w_turned.shape[1]
    return pl.pallas_call(
        backward_kernel,
        out_shape=(
            jax.ShapeDtypeStruct((rows, width), f32),
            jax.ShapeDtypeStruct((1, depth), f32),
            jax.ShapeDtypeStruct((2, 2, MAXSTEP * STAGES * rows, width // 2), bf16),
        ),
        in_specs=[SMEM, VMEM, ANY] + [VMEM] * 3,
        out_specs=(VMEM,) * 3,
        scratch_shapes=[pltpu.VMEM((rows, width), f32)] * 3 + [pltpu.SemaphoreType.DMA],
        compiler_params=packed_options(22),
        name="backward",
    )(info, given, following, ends, w_turned, tanhs)


def level_of(peak):
    return jnp.ceil(256.0 * jnp.log2(jnp.maximum(peak, 1e-30))) + 1.0


def scale_of(level):
    return jnp.exp2(level * (1.0 / 256.0) - 15.0)


def steps_of(level):
    return jnp.exp2(15.0 - level * (1.0 / 256.0))


def whole(values):
    return jnp.round(values).astype(jnp.int32).astype(jnp.int16)


def head_of(bias):
    level = level_of(jnp.abs(bias))
    steps = bias * steps_of(level)
    high = jnp.round(steps)
    return level, high, (steps - high) * TOP


def code_piece(low, high, head, store, store_head):
    shared = len(low)
    row = lax.broadcasted_iota(jnp.int32, (HEAD, LANES), 0)
    tile = jnp.zeros((HEAD, LANES), f32)
    for at, values in enumerate(head):
        tile = jnp.where(row == shared + at, values, tile)
    for block in range(shared):
        pair = (low[block](), high[block]())
        peak = jnp.maximum(jnp.abs(pair[0]), jnp.abs(pair[1]))
        level = level_of(jnp.max(peak, axis=0, keepdims=True))
        steps = steps_of(level)
        tile = jnp.where(row == block, level, tile)
        store(block, whole(pair[0] * steps))
        store(block + shared, whole(pair[1] * steps))
    store_head(whole(tile))


def code_kernel(batches, keep_low, keep_high, got_low, got_high, bias, message):
    turns = bias.shape[1] // LANES
    owners = batches // turns
    depth = keep_low.shape[0] // turns
    piece = depth // owners
    shared = keep_low.shape[1] // LANES

    def turn(i, carry):
        rows = pl.ds(pl.multiple_of(i * depth, depth), depth)
        stretch = bias[:, pl.ds(pl.multiple_of(i * LANES, LANES), LANES)]

        def sums(kept, got):
            return [
                functools.partial(lambda c: kept[rows, c] + got[rows, c], pl.ds(at * LANES, LANES))
                for at in range(shared)
            ]

        def store(block, numbers):
            for owner in range(owners):
                message[i * owners + owner, pl.ds(block * piece, piece), :] = numbers[
                    owner * piece : (owner + 1) * piece
                ]

        def store_head(numbers):
            for owner in range(owners):
                message[i * owners + owner, pl.ds(2 * shared * piece, HEAD), :] = numbers

        code_piece(
            sums(keep_low, got_low), sums(keep_high, got_high), head_of(stretch), store, store_head
        )
        return carry

    lax.fori_loop(0, turns, turn, 0)


def code(keep, received, bias, batches):
    depth, middle = keep[0].shape
    height = depth // batches * (2 * middle // LANES) + HEAD
    return pl.pallas_call(
        functools.partial(code_kernel, batches),
        out_shape=jax.ShapeDtypeStruct((batches, height, LANES), jnp.int16),
        in_specs=[VMEM] * 5,
        out_specs=VMEM,
        compiler_params=pltpu.CompilerParams(vmem_limit_bytes=16 * 1024 * 1024),
        name="code",
    )(*keep, *received, bias)


def read_piece(blocks, load):
    piece = blocks[0][1]
    shared = len(blocks) // 2
    head = load(len(blocks) * piece, HEAD).astype(jnp.int32).astype(f32)
    scale = scale_of(head)
    high, low = head[shared + 1 : shared + 2], head[shared + 2 : shared + 3]
    bias = (high + low * (1.0 / TOP)) * scale[shared : shared + 1]
    values = []
    for block, (at, rows) in enumerate(blocks):
        share = block % shared
        numbers = load(at, rows).astype(jnp.int32).astype(f32)
        values.append(numbers * scale[share : share + 1])
    return values, bias


def blocks_of(height, count):
    piece = (height - HEAD) // count
    return [(block * piece, piece) for block in range(count)]


def decode_kernel(count, message, out):
    senders, height, _ = message.shape
    blocks = blocks_of(height, count)
    group = 4

    def turn(i, carry):
        bias, *sums = carry
        for j in range(group):
            values, more = read_piece(
                blocks, lambda at, rows: message[i * group + j, pl.ds(at, rows), :]
            )
            bias = bias + more
            sums = [one + other for one, other in zip(sums, values)]
        return (bias, *sums)

    zeros = (jnp.zeros((1, LANES), f32),) + (jnp.zeros((blocks[0][1], LANES), f32),) * count
    bias, *sums = lax.fori_loop(0, senders // group, turn, zeros)
    ready = [functools.partial(lambda v: v, value) for value in sums]

    def store(block, numbers):
        at, rows = blocks[block]
        out[pl.ds(at, rows), :] = numbers

    def store_head(numbers):
        out[pl.ds(height - HEAD, HEAD), :] = numbers

    code_piece(ready[: count // 2], ready[count // 2 :], head_of(bias), store, store_head)


def decode(message, count):
    return pl.pallas_call(
        functools.partial(decode_kernel, count),
        out_shape=jax.ShapeDtypeStruct(message.shape[1:], jnp.int16),
        in_specs=[VMEM],
        out_specs=VMEM,
        compiler_params=pltpu.CompilerParams(vmem_limit_bytes=8 * 1024 * 1024),
        name="decode",
    )(message)


def lay_out_kernel(scale, info, mine, by_core, by_zlo, by_both, grad_in, grad_out, grad_bias):
    core, offset = info[0], info[1]
    count = grad_in.shape[1] // LANES
    blocks = blocks_of(mine.shape[0], count)
    parts = []
    stretches = []
    for ref in (mine, by_core, by_zlo, by_both):
        values, bias = read_piece(
            blocks, functools.partial(lambda r, at, rows: r[pl.ds(at, rows), :], ref)
        )
        parts.append(values)
        stretches.append(bias)

    def fill(kept, other):
        for block in range(count):
            columns = pl.ds(block * LANES, LANES)
            kept[:, columns] = (parts[0][block] + parts[2][block]) * scale
            other[:, columns] = (parts[1][block] + parts[3][block]) * scale

    @pl.when(core == 0)
    def _():
        fill(grad_in, grad_out)

    @pl.when(core == 1)
    def _():
        fill(grad_out, grad_in)

    stretch = ((stretches[0] + stretches[3]) + (stretches[1] + stretches[2])) * scale
    turned = pltpu.roll(jnp.broadcast_to(stretch, (8, LANES)), LANES - offset, 1)
    grad_bias[...] = turned[0:1, : grad_bias.shape[1]]


def lay_out(scale, info, quarters, rows, width):
    gradient = jax.ShapeDtypeStruct((rows, width), f32)
    return pl.pallas_call(
        functools.partial(lay_out_kernel, scale),
        out_shape=(gradient, gradient, jax.ShapeDtypeStruct((1, rows), f32)),
        in_specs=[SMEM] + [VMEM] * 4,
        out_specs=(VMEM,) * 3,
        compiler_params=pltpu.CompilerParams(vmem_limit_bytes=8 * 1024 * 1024),
        name="lay_out",
    )(info, *quarters)


def shrink_kernel(values, out):
    rows, width = values.shape
    columns = [pl.ds(at, LANES) for at in range(0, width, LANES)]
    loads = [functools.partial(lambda c: values[:, c], c) for c in columns]
    middle = len(loads) // 2

    def store(block, numbers):
        out[pl.ds(block * rows, rows), :] = numbers

    def store_head(numbers):
        out[pl.ds(2 * middle * rows, HEAD), :] = numbers

    code_piece(loads[:middle], loads[middle:], (), store, store_head)


def shrink(values):
    rows, width = values.shape
    return pl.pallas_call(
        shrink_kernel,
        out_shape=jax.ShapeDtypeStruct((rows * width // LANES + HEAD, LANES), jnp.int16),
        in_specs=[VMEM],
        out_specs=VMEM,
        compiler_params=pltpu.CompilerParams(vmem_limit_bytes=8 * 1024 * 1024),
        name="shrink",
    )(values)


def finish_kernel(info, bar, message, start, out):
    has_prev = info[0].astype(f32)
    blocks = blocks_of(message.shape[0], out.shape[1] // LANES)
    values, _ = read_piece(blocks, lambda at, rows: message[pl.ds(at, rows), :])
    for block, previous in enumerate(values):
        columns = pl.ds(block * LANES, LANES)
        gap = (previous - start[:, columns]) * has_prev
        out[:, columns] = bar[:, columns] - penalty * gap


def finish(info, bar, message, start):
    return pl.pallas_call(
        finish_kernel,
        out_shape=jax.ShapeDtypeStruct(bar.shape, f32),
        in_specs=[SMEM] + [VMEM] * 3,
        out_specs=VMEM,
        compiler_params=pltpu.CompilerParams(vmem_limit_bytes=8 * 1024 * 1024),
        name="finish",
    )(info, bar, message, start)


def contract_rows(left, right):
    return lax.dot_general(left, right, (((0,), (0,)), ((), ())), preferred_element_type=f32)


def shift_seg(block, distance):
    count = lax.axis_size(SEG)
    route = [(i - distance, i) for i in range(count) if 0 <= i - distance < count]
    return lax.ppermute(block, SEG, route)


def swap(block):
    return lax.ppermute(block, "core", [(0, 1), (1, 0)])


def body(starts, targets, counts, w_in, b_in, w_out):
    start = starts[0]
    core = lax.axis_index("core")
    place = lax.axis_index(SEG)
    batches = lax.axis_size("batch")
    rows, width = start.shape
    own = w_in.shape[0]

    following = shift_seg(start, -1)
    shard = jnp.where(core == 0, w_in, w_out)
    copies = jnp.broadcast_to(shard[None], (batches, own, width))
    own_w = lax.all_to_all(copies, "batch", 0, 0)
    own_w = own_w.reshape(batches * own, width)
    other_w = swap(own_w)
    given = jnp.stack([start, targets[0]])

    has_next = (place < lax.axis_size(SEG) - 1).astype(jnp.int32)
    info = jnp.stack([counts[0], core, has_next])
    ends, left, w_turned, tanhs = forward(info, given, b_in[None], own_w, other_w)
    bar, bias, right = backward(info, given, pltpu.with_memory_space_constraint(following, pltpu.HBM), ends, w_turned, tanhs)
    small = shrink(ends)
    previous = shift_seg(small, 1)
    has_prev = (place > 0).astype(jnp.int32)
    grad_starts = finish(has_prev[None], bar, previous, start)[None]

    received, keep = [], []
    for half in range(2):
        sent = contract_rows(left[0], right[0, half])
        received.append(swap(sent))
    for half in range(2):
        keep.append(contract_rows(left[1], right[1, half]))
    message = code(keep, received, bias, batches)
    message = lax.all_to_all(message, "batch", 0, 0)
    mine = decode(message, width // LANES)
    quarters = [mine] + [
        lax.ppermute(mine, SEG, [(i, i ^ flip) for i in range(4)]) for flip in (1, 2, 3)
    ]
    offset = lax.axis_index("batch") % (LANES // own) * own
    scale = 1.0 / math.sqrt(rows * batches)
    grad_in, grad_out, grad_bias = lay_out(scale, jnp.stack([core, offset]), quarters, own, width)
    return (grad_starts, grad_in, grad_out, grad_bias[0])


def solution(mesh):
    segs, batches = mesh.devices.shape
    finer = Mesh(mesh.devices.reshape(2, segs // 2, batches), ("zlo", "core", "batch"))
    return jax.shard_map(
        body,
        mesh=finer,
        in_specs=(
            P(SEG, "batch", None),
            P(SEG, "batch", None),
            P(SEG),
            P("batch", None),
            P(),
            P("batch", None),
        ),
        out_specs=(P(SEG, "batch", None), P("batch", None), P("batch", None), P("batch")),
        check_vma=False,
    )
```
